32 devices in a mesh: parts: 2 (over x), seq: 16 (over z, y, core).
Axes of the slice: x: 2, y: 2, z: 4, core: 2. Of those that a mesh axis runs over, the one named last changes fastest.
Arguments:
- queries: bfloat16 [16384, 2048], P(('parts', 'seq')), parts along dimension 0, may hold values from -100 to 100
- out_grad: bfloat16 [16384, 2048], P(('parts', 'seq')), parts along dimension 0, may hold values from -6 to 6
- query_mask: int32 [16384], P(('parts', 'seq')), parts along dimension 0, may hold values 0 or 1
- enc_hidden: bfloat16 [128, 1024], P(('parts', 'seq')), parts along dimension 0, may hold values from -6 to 6
- norm_gain: bfloat16 [1024], replicated, may hold values from 0.099609375 to 1.8984375
- key_weight: bfloat16 [1024, 2048], replicated, may hold values from -0.1875 to 0.1875
- value_weight: bfloat16 [1024, 2048], replicated, may hold values from -0.1875 to 0.1875
- mem_len: int32 [32], P('parts'), parts along dimension 0, may hold values from 1 to 4, as said below
Outputs:
- query_grad: bfloat16 [16384, 2048], P(('parts', 'seq')), parts along dimension 0
- hidden_grad: bfloat16 [128, 1024], P(('parts', 'seq')), parts along dimension 0
The draws below stay inside these ranges and needn't reach their ends.
There are 2 independent parts, one for each index of `parts`. The reference program is written for one: setup_inputs(seed, part) draws one part's arguments, and reference() takes and returns one part's arrays. A program takes and returns all parts, laid end to end along the dimension named above; an argument that names none is the same for every part. Nothing has to cross between parts.
Inputs may be any that keep to these rules, and one draw needn't show every extreme that they name: `mem_len`: the live slots stand at the head of each group of 4; some group is full.
All inputs are finite; a program needn't handle non-finite values. No bound on the sum of `query_mask` on one device may be relied on, other than what follows from the above.
Results may differ from the reference program's by a relative error of at most 0.02.
Values may be sent and summed in bfloat16 or wider, within the bound.
No kernel may reach another device: no remote copies, remote signals or barrier semaphores. Data moves between devices by JAX's collectives and lax.ppermute only.
A program may use at most 128 MiB of HBM per device.

```python
import math
import jax
import jax.numpy as jnp
from jax import lax

HEADS = 16
HD = 128
D_ENC = 1024
M_DEV = 4
QTOK = 8192
MEM = 64
GROUPS = 16


def draw_queries(key, part):
    return jnp.clip(jax.random.normal(key, (QTOK, HEADS * HD), jnp.float32), -6.0, 6.0).astype(jnp.bfloat16)


def draw_mem_len(key, part):
    length_key, index_key = jax.random.split(jax.random.fold_in(key, 7))
    lengths = jax.random.randint(length_key, (GROUPS,), 1, M_DEV + 1)
    full_index = jax.random.randint(index_key, (), 0, GROUPS)
    return lengths.at[full_index].set(M_DEV).astype(jnp.int32)


def place_ends(result, rng, low, high):
    extent = result.shape
    place = [jax.random.randint(jax.random.fold_in(rng, axis), (), 0, extent[axis]) for axis in range(len(extent))]
    result = result.at[tuple(place)].set(low)
    longest = extent.index(max(extent))
    place[longest] = (place[longest] + 1) % extent[longest]
    return result.at[tuple(place)].set(high)


def level_of(own_key, shape, cuts, low, top_value):
    def one(axis_at, parts):
        draws = jax.random.uniform(jax.random.fold_in(jax.random.fold_in(own_key, 6), axis_at), (parts,), jnp.float32, low / len(cuts), top_value / len(cuts))
        return jnp.repeat(jnp.exp(draws), shape[axis_at] // parts).reshape((-1,) + (1,) * (len(shape) - axis_at - 1))

    factor_of = one(*cuts[0])
    for cut in cuts[1:]:
        factor_of = factor_of * one(*cut)
    return factor_of


def gaussian(own_key, shape, spread, reach, cuts=(), held_as=jnp.bfloat16):
    result = jax.random.normal(own_key, shape, jnp.float32) * spread
    if len(cuts) > 0:
        result = level_of(own_key, shape, cuts, -0.22, 0.18) * result
    return jnp.clip(result, min=-reach, max=reach).astype(held_as)


def setup_inputs(seed: int = 0, part: int = 0) -> dict:
    key_list = jax.random.split(jax.random.key(seed), 9)
    part_splits = jax.random.split(jax.random.fold_in(key_list[8], part), 9)
    return {
        "queries": draw_queries(jax.random.fold_in(jax.random.fold_in(key_list[8], part), 71), part),
        "out_grad": gaussian(part_splits[1], (QTOK, HEADS * HD), 1.0, 6.0, ((0, 16),)),
        "query_mask": place_ends((jax.random.randint(part_splits[2], (QTOK,), 0, 8) < 7).astype(jnp.int32), jax.random.fold_in(part_splits[2], 1), 0, 1),
        "enc_hidden": gaussian(part_splits[3], (MEM, D_ENC), 1.0, 6.0, ((0, 16),)),
        "norm_gain": jnp.clip(1.0 + 0.18 * jax.random.normal(key_list[4], (D_ENC,), jnp.float32), 0.099609375, 1.8984375).astype(jnp.bfloat16),
        "key_weight": gaussian(key_list[5], (D_ENC, HEADS * HD), D_ENC ** -0.5, 0.1875),
        "value_weight": gaussian(key_list[6], (D_ENC, HEADS * HD), D_ENC ** -0.5, 0.1875),
        "mem_len": draw_mem_len(jax.random.fold_in(jax.random.fold_in(key_list[8], part), 71), part),
    }


def normalize(enc_hidden, norm_gain):
    hidden_f = enc_hidden.astype(jnp.float32)
    inverse_rms = lax.rsqrt(lax.optimization_barrier(jnp.mean(hidden_f * hidden_f, axis=-1, keepdims=True)) + 1e-05)
    memory = (hidden_f * inverse_rms * norm_gain.astype(jnp.float32)).astype(jnp.bfloat16)
    return (memory, inverse_rms)

def live_slots(mem_len, slot_count):
    offsets = jnp.arange(slot_count, dtype=jnp.int32)
    return (offsets[None, :] < mem_len[:, None].astype(jnp.int32)).reshape(-1)

def norm_backward(enc_hidden, norm_gain, inverse_rms, norm_grad):
    hidden_f = enc_hidden.astype(jnp.float32)
    normed = hidden_f * inverse_rms
    scaled = norm_grad * norm_gain.astype(jnp.float32)
    inner_mean = lax.optimization_barrier(jnp.mean(scaled * normed, axis=-1, keepdims=True))
    return (inverse_rms * (scaled - normed * inner_mean)).astype(jnp.bfloat16)

def reference(queries, out_grad, query_mask, enc_hidden, norm_gain, key_weight, value_weight, mem_len):
    score_scale = 1.0 / math.sqrt(HD)
    memory, inverse_rms = normalize(enc_hidden, norm_gain)
    key_rows = jnp.dot(memory, key_weight, preferred_element_type=jnp.float32).astype(jnp.bfloat16)
    value_rows = jnp.dot(memory, value_weight, preferred_element_type=jnp.float32).astype(jnp.bfloat16)
    live = live_slots(mem_len, M_DEV)
    grad_rows = out_grad * query_mask[:, None].astype(jnp.bfloat16)

    def by_head(matrix):
        return matrix.reshape(matrix.shape[0], HEADS, HD).transpose(1, 0, 2)

    def one_head(operands):
        query_head, key_head, value_head, grad_head = operands
        scores = jnp.dot(query_head, key_head.T, preferred_element_type=jnp.float32) * score_scale
        scores = jnp.where(live[None, :], scores, -jnp.inf)
        exponent = jnp.exp(scores - lax.optimization_barrier(jnp.max(scores, axis=-1, keepdims=True)))
        attention = exponent / lax.optimization_barrier(jnp.sum(exponent, axis=-1, keepdims=True))
        attention_b = attention.astype(jnp.bfloat16)
        head_out = jnp.dot(attention_b, value_head, preferred_element_type=jnp.float32)
        delta = lax.optimization_barrier(jnp.sum(grad_head.astype(jnp.float32) * head_out, axis=-1, keepdims=True))
        grad_scores = jnp.dot(grad_head, value_head.T, preferred_element_type=jnp.float32)
        score_grad = (attention * (grad_scores - delta)).astype(jnp.bfloat16)
        query_part = (jnp.dot(score_grad, key_head, preferred_element_type=jnp.float32) * score_scale).astype(jnp.bfloat16)
        key_part = jnp.dot(score_grad.T, query_head, preferred_element_type=jnp.float32) * score_scale
        value_part = jnp.dot(attention_b.T, grad_head, preferred_element_type=jnp.float32)
        return (query_part, key_part, value_part)
    query_heads, key_heads, value_heads = lax.map(one_head, (by_head(queries), by_head(key_rows), by_head(value_rows), by_head(grad_rows)))
    query_grad = query_heads.transpose(1, 0, 2).reshape(QTOK, HEADS * HD)
    key_grad = key_heads.transpose(1, 0, 2).reshape(MEM, HEADS * HD)
    value_grad = value_heads.transpose(1, 0, 2).reshape(MEM, HEADS * HD)
    norm_grad = jnp.dot(key_grad, key_weight.astype(jnp.float32).T, precision=lax.Precision.HIGHEST)
    norm_grad = norm_grad + jnp.dot(value_grad, value_weight.astype(jnp.float32).T, precision=lax.Precision.HIGHEST)
    hidden_grad = norm_backward(enc_hidden, norm_gain, inverse_rms, norm_grad)
    return (query_grad, hidden_grad)
```

```python
import functools
import math

import jax
import jax.numpy as jnp
from jax import lax
from jax.experimental import pallas as pl
from jax.experimental.pallas import tpu as pltpu
from jax.sharding import PartitionSpec as P

HEADS = 16
HD = 128
STEP_HEADS = 2
SCALE = 1.0 / math.sqrt(HD)
LOG2E = 1.4426950408889634


def exchange(array, distance, size):
    return lax.ppermute(array, "seq", [(i, i ^ distance) for i in range(size)])


def owner_offset(index, bits):
    offset = 0
    for bit in range(bits):
        offset |= ((index >> bit) & 1) << (bits - 1 - bit)
    return offset


def nt(a, b):
    return lax.dot_general(a, b, (((1,), (1,)), ((), ())), preferred_element_type=jnp.float32)


def nn(a, b):
    return lax.dot_general(a, b, (((1,), (0,)), ((), ())), preferred_element_type=jnp.float32)


def tn(a, b):
    return lax.dot_general(a, b, (((0,), (0,)), ((), ())), preferred_element_type=jnp.float32)


def attention_kernel(
    rows, bits, len_ref, hid_ref, gain_ref, mask_ref, q_ref, g_ref, kw_ref, vw_ref,
    part_ref, qg_ref, mem_ref, bias_ref, acc_ref,
):
    step = pl.program_id(0)
    slots = hid_ref.shape[0]

    @pl.when(step == 0)
    def _():
        hidden = hid_ref[...].astype(jnp.float32)
        inverse_rms = lax.rsqrt(jnp.mean(hidden * hidden, axis=-1, keepdims=True) + 1e-05)
        gain = gain_ref[...].astype(jnp.float32)
        mem_ref[...] = (hidden * inverse_rms * gain).astype(jnp.bfloat16)
        me = lax.axis_index("seq")
        row = lax.broadcasted_iota(jnp.int32, (slots, HD), 0)
        group = row // rows
        length = jnp.zeros((slots, HD), jnp.int32)
        for index in range(slots // rows):
            length = jnp.where(group == index, len_ref[me ^ owner_offset(index, bits)], length)
        bias_ref[...] = jnp.where(row - group * rows < length, 0.0, -jnp.inf)
        acc_ref[...] = jnp.zeros_like(acc_ref)

    memory = mem_ref[...]
    keys = nn(memory, kw_ref[...]).astype(jnp.bfloat16)
    values = nn(memory, vw_ref[...]).astype(jnp.bfloat16)
    tokens = q_ref.shape[0]
    bias = jnp.concatenate([bias_ref[...]] * (tokens // HD), axis=1)
    real = mask_ref[...].astype(jnp.float32)
    key_parts, value_parts = [], []
    for head in range(q_ref.shape[1] // HD):
        at = slice(head * HD, (head + 1) * HD)
        query, grad, key, value = q_ref[:, at], g_ref[:, at], keys[:, at], values[:, at]
        scores = nt(key, query) + bias
        top = jnp.max(scores, axis=0, keepdims=True)
        exponent = jnp.exp2((scores - top) * (SCALE * LOG2E))
        attention = exponent * (real / jnp.sum(exponent, axis=0, keepdims=True))
        grad_scores = nt(value, grad)
        delta = jnp.sum(attention * grad_scores, axis=0, keepdims=True)
        score_grad = (attention * ((grad_scores - delta) * SCALE)).astype(jnp.bfloat16)
        qg_ref[:, at] = tn(score_grad, key).astype(jnp.bfloat16)
        key_parts.append(nn(score_grad, query).astype(jnp.bfloat16))
        value_parts.append(nn(attention.astype(jnp.bfloat16), grad).astype(jnp.bfloat16))
    acc_ref[...] += nt(jnp.concatenate(key_parts, axis=1), kw_ref[...]) + nt(
        jnp.concatenate(value_parts, axis=1), vw_ref[...]
    )

    @pl.when(step == pl.num_programs(0) - 1)
    def _():
        part_ref[...] = acc_ref[...]


def attention_call(rows, bits, mem_len, hidden, gain, mask, queries, out_grad, key_weight, value_weight):
    slots, width = hidden.shape
    tokens, columns = queries.shape
    wide = STEP_HEADS * HD
    whole = lambda *shape: pl.BlockSpec(shape, lambda i: (0,) * len(shape))
    column = lambda n: pl.BlockSpec((n, wide), lambda i: (0, i))
    return pl.pallas_call(
        functools.partial(attention_kernel, rows, bits),
        grid=(columns // wide,),
        in_specs=[
            pl.BlockSpec(memory_space=pltpu.SMEM),
            whole(slots, width),
            whole(1, width),
            whole(1, tokens),
            column(tokens),
            column(tokens),
            column(width),
            column(width),
        ],
        out_specs=[whole(slots, width), column(tokens)],
        out_shape=[
            jax.ShapeDtypeStruct((slots, width), jnp.float32),
            jax.ShapeDtypeStruct((tokens, columns), jnp.bfloat16),
        ],
        scratch_shapes=[
            pltpu.VMEM((slots, width), jnp.bfloat16),
            pltpu.VMEM((slots, HD), jnp.float32),
            pltpu.VMEM((slots, width), jnp.float32),
        ],
        name="attention_backward",
    )(mem_len, hidden, gain, mask, queries, out_grad, key_weight, value_weight)


def norm_kernel(own_ref, other_ref, hid_ref, gain_ref, out_ref):
    norm_grad = own_ref[...] + other_ref[...].astype(jnp.float32)
    hidden = hid_ref[...].astype(jnp.float32)
    inverse_rms = lax.rsqrt(jnp.mean(hidden * hidden, axis=-1, keepdims=True) + 1e-05)
    normed = hidden * inverse_rms
    scaled = norm_grad * gain_ref[...].astype(jnp.float32)
    inner_mean = jnp.mean(scaled * normed, axis=-1, keepdims=True)
    out_ref[...] = (inverse_rms * (scaled - normed * inner_mean)).astype(jnp.bfloat16)


def shards(size, queries, out_grad, query_mask, enc_hidden, norm_gain, key_weight, value_weight, mem_len):
    rows, width = enc_hidden.shape
    bits = size.bit_length() - 1
    gain = norm_gain.reshape(1, width)
    gathered = enc_hidden[None]
    for bit in reversed(range(bits)):
        gathered = jnp.concatenate([gathered, exchange(gathered, 1 << bit, size)], axis=0)
    partial, query_grad = attention_call(
        rows, bits, mem_len, gathered.reshape(size * rows, width), gain, query_mask.reshape(1, -1),
        queries, out_grad, key_weight, value_weight,
    )
    kept = partial.reshape(size, rows, width)
    for bit in range(bits):
        half = kept.shape[0] // 2
        received = exchange(kept[half:].astype(jnp.bfloat16), 1 << bit, size)
        if bit < bits - 1:
            kept = kept[:half] + received.astype(jnp.float32)
    hidden_grad = pl.pallas_call(
        norm_kernel,
        out_shape=jax.ShapeDtypeStruct((rows, width), jnp.bfloat16),
        name="norm_backward",
    )(kept[0], received[0], enc_hidden, gain)
    return (query_grad, hidden_grad)


def solution(mesh):
    in_specs = (
        P(("parts", "seq"), None),
        P(("parts", "seq"), None),
        P(("parts", "seq")),
        P(("parts", "seq"), None),
        P(),
        P(),
        P(),
        P("parts"),
    )
    out_specs = (P(("parts", "seq"), None), P(("parts", "seq"), None))
    body = functools.partial(shards, mesh.shape["seq"])
    return jax.shard_map(body, mesh=mesh, in_specs=in_specs, out_specs=out_specs, check_vma=False)
```

```python
import functools
import math

import jax
import jax.numpy as jnp
from jax import lax
from jax.experimental import pallas as pl
from jax.experimental.pallas import tpu as pltpu
from jax.sharding import PartitionSpec as P

HD = 128
CHUNK = 256
SCALE = 1.0 / math.sqrt(HD)
LOG2E = 1.4426950408889634
IN_VMEM = pl.BlockSpec(memory_space=pltpu.VMEM)


def exchange(array, distance, size):
    return lax.ppermute(array, "seq", [(i, i ^ distance) for i in range(size)])


def owner_offset(index, bits):
    offset = 0
    for bit in range(bits):
        offset |= ((index >> bit) & 1) << (bits - 1 - bit)
    return offset


def nt(a, b):
    return lax.dot_general(a, b, (((1,), (1,)), ((), ())), preferred_element_type=jnp.float32)


def nn(a, b):
    return lax.dot_general(a, b, (((1,), (0,)), ((), ())), preferred_element_type=jnp.float32)


def tn(a, b):
    return lax.dot_general(a, b, (((0,), (0,)), ((), ())), preferred_element_type=jnp.float32)


def small_vmem(mebibytes):
    return pltpu.CompilerParams(vmem_limit_bytes=mebibytes * 2**20)


def to_vmem(array):
    return pltpu.with_memory_space_constraint(array, pltpu.VMEM)


def load_kernel(pieces, src_ref, dst_ref, sems):
    rows = src_ref.shape[0] // pieces
    copies = [
        pltpu.make_async_copy(src_ref.at[pl.ds(i * rows, rows)], dst_ref.at[pl.ds(i * rows, rows)], sems.at[i])
        for i in range(pieces)
    ]
    for copy in copies:
        copy.start()
    for copy in copies:
        copy.wait()


def load_call(array, pieces=4):
    return pl.pallas_call(
        functools.partial(load_kernel, pieces),
        in_specs=[pl.BlockSpec(memory_space=pltpu.HBM)],
        out_specs=IN_VMEM,
        out_shape=pltpu.VMEM(array.shape, array.dtype),
        scratch_shapes=[pltpu.SemaphoreType.DMA((pieces,))],
        compiler_params=small_vmem(1),
        name="load",
    )(pltpu.with_memory_space_constraint(array, pltpu.HBM))


def setup_kernel(rows, bits, len_ref, mask_ref, gain_ref, hid_ref, bias_ref, real_ref, gain_out, hid_out):
    slots = bias_ref.shape[0]
    me = lax.axis_index("seq")
    row = lax.broadcasted_iota(jnp.int32, (slots, HD), 0)
    group = row // rows
    length = jnp.zeros((slots, HD), jnp.int32)
    for index in range(slots // rows):
        length = jnp.where(group == index, len_ref[me ^ owner_offset(index, bits)], length)
    bias_ref[...] = jnp.where(row - group * rows < length, 0.0, -jnp.inf)
    real_ref[...] = mask_ref[...].astype(jnp.float32)
    gain_out[...] = gain_ref[...].astype(jnp.float32)
    hid_out[...] = hid_ref[...].astype(jnp.float32)


def setup_call(rows, bits, slots, mem_len, mask, gain, hidden):
    return pl.pallas_call(
        functools.partial(setup_kernel, rows, bits),
        in_specs=[pl.BlockSpec(memory_space=pltpu.SMEM)] + [pl.BlockSpec()] * 3,
        out_specs=[IN_VMEM] * 4,
        out_shape=[
            pltpu.VMEM((slots, HD), jnp.float32),
            pltpu.VMEM(mask.shape, jnp.float32),
            pltpu.VMEM(gain.shape, jnp.float32),
            pltpu.VMEM(hidden.shape, jnp.float32),
        ],
        compiler_params=small_vmem(2),
        name="setup",
    )(mem_len, mask, gain, hidden)


def attention_kernel(
    near_ref, far_ref, gain_ref, bias_ref, real_ref, q_ref, g_ref, kw_ref, vw_ref,
    send_ref, keep_ref, sg_ref, key_ref, value_ref, att_ref, kg_ref, vg_ref,
):
    half = near_ref.shape[0]
    slots = 2 * half
    tokens, columns = q_ref.shape
    heads = columns // HD
    hidden = jnp.concatenate([near_ref[...], far_ref[...]], axis=0).astype(jnp.float32)
    inverse_rms = lax.rsqrt(jnp.mean(hidden * hidden, axis=-1, keepdims=True) + 1e-05)
    memory = (hidden * inverse_rms * gain_ref[...]).astype(jnp.bfloat16)
    bias = jnp.concatenate([bias_ref[...]] * (CHUNK // HD), axis=1)
    real = real_ref[...]

    def project(pair):
        at = slice(pair * 2 * HD, (pair + 1) * 2 * HD)
        key_ref[:, at] = nn(memory, kw_ref[:, at]).astype(jnp.bfloat16)
        value_ref[:, at] = nn(memory, vw_ref[:, at]).astype(jnp.bfloat16)

    def softmax(head):
        at, here = slice(head * HD, (head + 1) * HD), slice(head * slots, (head + 1) * slots)
        for chunk in range(tokens // CHUNK):
            part = slice(chunk * CHUNK, (chunk + 1) * CHUNK)
            scores = nt(key_ref[:, at], q_ref[part, at]) + bias
            grad_scores = nt(value_ref[:, at], g_ref[part, at])
            top = jnp.max(scores, axis=0, keepdims=True)
            exponent = jnp.exp2((scores - top) * (SCALE * LOG2E))
            attention = exponent * (real[:, part] / jnp.sum(exponent, axis=0, keepdims=True))
            delta = jnp.sum(attention * grad_scores, axis=0, keepdims=True)
            sg_ref[here, part] = (attention * (grad_scores - delta)).astype(jnp.bfloat16)
            att_ref[head % 4, :, part] = attention.astype(jnp.bfloat16)

    def product(head):
        at, here = slice(head * HD, (head + 1) * HD), slice(head * slots, (head + 1) * slots)
        kg_ref[:, at] = (nn(sg_ref[here, :], q_ref[:, at]) * SCALE).astype(jnp.bfloat16)
        vg_ref[:, at] = nn(att_ref[head % 4], g_ref[:, at]).astype(jnp.bfloat16)

    project(0)
    for head in range(heads):
        if head % 2 == 0 and head + 2 < heads:
            project(head // 2 + 1)
        softmax(head)
        if head > 0:
            product(head - 1)
    product(heads - 1)
    partial = nt(kg_ref[...], kw_ref[...]) + nt(vg_ref[...], vw_ref[...])
    keep_ref[...] = partial[:half]
    send_ref[...] = partial[half:].astype(jnp.bfloat16)


def attention_call(near, far, gain, bias, real, queries, out_grad, key_weight, value_weight):
    half, width = near.shape
    slots = 2 * half
    tokens, columns = queries.shape
    heads = columns // HD
    scratch = lambda *shape: pltpu.VMEM(shape, jnp.bfloat16)
    operands = [near, far, gain, bias, real, queries, out_grad, key_weight, value_weight]
    return pl.pallas_call(
        attention_kernel,
        in_specs=[IN_VMEM] * len(operands),
        out_specs=[IN_VMEM] * 4,
        out_shape=[
            pltpu.VMEM((half, width), jnp.bfloat16),
            pltpu.VMEM((half, width), jnp.float32),
            pltpu.VMEM((heads * slots, tokens), jnp.bfloat16),
            pltpu.VMEM((slots, columns), jnp.bfloat16),
        ],
        scratch_shapes=[
            scratch(slots, columns),
            scratch(4, slots, tokens),
            scratch(slots, columns),
            scratch(slots, columns),
        ],
        compiler_params=small_vmem(8 + 2 * slots * columns * 10 // 2**20),
        name="attention_backward",
    )(*[to_vmem(x) for x in operands])


def query_kernel(first, heads, sg_ref, key_ref, *refs):
    out_ref, block_ref, sems = refs[-3:]
    slots = key_ref.shape[0]
    copies = []
    for index in range(heads):
        head = first + index
        at, here = slice(head * HD, (head + 1) * HD), slice(head * slots, (head + 1) * slots)
        block_ref[index] = (tn(sg_ref[here, :], key_ref[:, at]) * SCALE).astype(jnp.bfloat16)
        copies.append(pltpu.make_async_copy(block_ref.at[index], out_ref.at[:, at], sems.at[index]))
        copies[-1].start()
    for copy in copies:
        copy.wait()


def query_call(first, heads, score_grad, keys, so_far):
    columns = keys.shape[1]
    tokens = score_grad.shape[1]
    before = [] if so_far is None else [so_far]
    return pl.pallas_call(
        functools.partial(query_kernel, first, heads),
        in_specs=[IN_VMEM] * 2 + [pl.BlockSpec(memory_space=pl.ANY)] * len(before),
        out_specs=pl.BlockSpec(memory_space=pl.ANY),
        out_shape=jax.ShapeDtypeStruct((tokens, columns), jnp.bfloat16),
        scratch_shapes=[
            pltpu.VMEM((heads, tokens, HD), jnp.bfloat16),
            pltpu.SemaphoreType.DMA((heads,)),
        ],
        input_output_aliases={2: 0} if before else {},
        compiler_params=small_vmem(8),
        name="query_grad",
    )(to_vmem(score_grad), to_vmem(keys), *before)


def norm_kernel(own_ref, other_ref, hid_ref, gain_ref, out_ref):
    norm_grad = own_ref[...] + other_ref[...].astype(jnp.float32)
    hidden = hid_ref[...]
    inverse_rms = lax.rsqrt(jnp.mean(hidden * hidden, axis=-1, keepdims=True) + 1e-05)
    normed = hidden * inverse_rms
    scaled = norm_grad * gain_ref[...]
    inner_mean = jnp.mean(scaled * normed, axis=-1, keepdims=True)
    out_ref[...] = (inverse_rms * (scaled - normed * inner_mean)).astype(jnp.bfloat16)


def shards(size, queries, out_grad, query_mask, enc_hidden, norm_gain, key_weight, value_weight, mem_len):
    rows, width = enc_hidden.shape
    bits = size.bit_length() - 1
    heads = queries.shape[1] // HD
    setup = lambda *given: setup_call(rows, bits, size * rows, *given)
    small = (mem_len, query_mask.reshape(1, -1), norm_gain.reshape(1, width), enc_hidden)
    early = [[(load_call, queries), (setup, *small)], [(load_call, key_weight)], [(load_call, value_weight)], [(load_call, out_grad)]]
    ready = []
    near = enc_hidden
    for step in range(bits):
        far = exchange(near, size >> (step + 1), size)
        for call, *given in early[step] if step < len(early) else []:
            given = lax.optimization_barrier((near, *given))[1:] if step else given
            ready.append(call(*given))
            far, ready[-1] = lax.optimization_barrier((far, ready[-1]))
        if step < bits - 1:
            near = lax.optimization_barrier(jnp.concatenate([near, far], axis=0))
    ready += [call(*given) for step in early[bits:] for call, *given in step]
    loaded_queries, (bias, real, gain, hidden), loaded_key, loaded_value, loaded_grad = ready
    send, keep, score_grad, keys = attention_call(
        near, far, gain, bias, real, loaded_queries, loaded_grad, loaded_key, loaded_value
    )
    query_grad = None
    shares = [(1, 0, 6), (2, 6, 5), (3, 11, 5)]
    for bit in range(bits):
        received = exchange(send, 1 << bit, size)
        for at, first, count in shares:
            if at == bit:
                score_grad, send = lax.optimization_barrier((score_grad, send))
                query_grad = query_call(first, count, score_grad, keys, query_grad)
                received, query_grad = lax.optimization_barrier((received, query_grad))
        if bit < bits - 1:
            half = keep.shape[0] // 2
            total = keep + received.astype(jnp.float32)
            keep, send = total[:half], total[half:].astype(jnp.bfloat16)
    operands = [keep, received, hidden, gain]
    hidden_grad = pl.pallas_call(
        norm_kernel,
        in_specs=[IN_VMEM] * 4,
        out_specs=IN_VMEM,
        out_shape=jax.ShapeDtypeStruct((rows, width), jnp.bfloat16),
        compiler_params=small_vmem(2),
        name="norm_backward",
    )(*[to_vmem(x) for x in operands])
    return (query_grad, hidden_grad)


def solution(mesh):
    in_specs = (
        P(("parts", "seq"), None),
        P(("parts", "seq"), None),
        P(("parts", "seq")),
        P(("parts", "seq"), None),
        P(),
        P(),
        P(),
        P("parts"),
    )
    out_specs = (P(("parts", "seq"), None), P(("parts", "seq"), None))
    body = functools.partial(shards, mesh.shape["seq"])
    return jax.shard_map(body, mesh=mesh, in_specs=in_specs, out_specs=out_specs, check_vma=False)
```

```python
import functools
import math

import jax
import jax.numpy as jnp
from jax import lax
from jax.experimental import pallas as pl
from jax.experimental.pallas import tpu as pltpu
from jax.sharding import PartitionSpec as P

HD = 128
CHUNK = 256
SCALE = 1.0 / math.sqrt(HD)
LOG2E = 1.4426950408889634
IN_VMEM = pl.BlockSpec(memory_space=pltpu.VMEM)
IN_HBM = pl.BlockSpec(memory_space=pltpu.HBM)
WIDE = 2 * HD


def exchange(array, distance, size):
    return lax.ppermute(array, "seq", [(i, i ^ distance) for i in range(size)])


def owner_offset(index, bits):
    offset = 0
    for bit in range(bits):
        offset |= ((index >> bit) & 1) << (bits - 1 - bit)
    return offset


def nt(a, b):
    return lax.dot_general(a, b, (((1,), (1,)), ((), ())), preferred_element_type=jnp.float32)


def nn(a, b):
    return lax.dot_general(a, b, (((1,), (0,)), ((), ())), preferred_element_type=jnp.float32)


def tn(a, b):
    return lax.dot_general(a, b, (((0,), (0,)), ((), ())), preferred_element_type=jnp.float32)


def small_vmem(mebibytes):
    return pltpu.CompilerParams(vmem_limit_bytes=mebibytes * 2**20)


def to_vmem(array):
    return pltpu.with_memory_space_constraint(array, pltpu.VMEM)


def column_copies(first, sources, targets, sems):
    copies = []
    for index, (source, target) in enumerate(zip(sources, targets)):
        rows, columns = target.shape
        for half in range(2):
            at = slice(half * rows // 2, (half + 1) * rows // 2)
            copies.append(
                pltpu.make_async_copy(
                    source.at[at, first : first + columns], target.at[at], sems.at[2 * index + half]
                )
            )
    return copies


def load_kernel(first, *refs):
    copies = column_copies(first, refs[:4], refs[4:8], refs[8])
    for copy in copies:
        copy.start()
    for copy in copies:
        copy.wait()


def in_hbm(arrays):
    return [pltpu.with_memory_space_constraint(x, pltpu.HBM) for x in arrays]


def column_shapes(arrays, columns):
    return [pltpu.VMEM((x.shape[0], columns), x.dtype) for x in arrays]


def load_call(first, columns, *arrays):
    return pl.pallas_call(
        functools.partial(load_kernel, first),
        in_specs=[IN_HBM] * 4,
        out_specs=[IN_VMEM] * 4,
        out_shape=column_shapes(arrays, columns),
        scratch_shapes=[pltpu.SemaphoreType.DMA((8,))],
        compiler_params=small_vmem(1),
        name="load",
    )(*in_hbm(arrays))


def setup_kernel(rows, bits, first, *refs):
    small, refs = refs[:4], refs[4:]
    sources, (bias_ref, real_ref, gain_out, hid_out), targets = refs[:4], refs[4:8], refs[8:12]
    held, small_sems, sems = refs[12:16], refs[16], refs[17]
    near = [pltpu.make_async_copy(small[i], held[i], small_sems.at[i]) for i in range(4)]
    copies = column_copies(first, sources, targets, sems)
    for copy in near + copies:
        copy.start()
    for copy in near:
        copy.wait()
    len_ref, mask_ref, gain_ref, hid_ref = held
    slots = bias_ref.shape[0]
    me = lax.axis_index("seq")
    row = lax.broadcasted_iota(jnp.int32, (slots, HD), 0)
    group = row // rows
    length = jnp.zeros((slots, HD), jnp.int32)
    for index in range(slots // rows):
        length = jnp.where(group == index, len_ref[me ^ owner_offset(index, bits)], length)
    bias_ref[...] = jnp.where(row - group * rows < length, 0.0, -jnp.inf)
    real_ref[...] = mask_ref[...].astype(jnp.float32)
    gain_out[...] = gain_ref[...].astype(jnp.float32).reshape(1, -1)
    hid_out[...] = hid_ref[...].astype(jnp.float32)
    for copy in copies:
        copy.wait()


def setup_call(rows, bits, slots, first, columns, mem_len, mask, gain, hidden, *arrays):
    small = (mem_len, mask, gain, hidden)
    return pl.pallas_call(
        functools.partial(setup_kernel, rows, bits, first),
        in_specs=[IN_HBM] * 8,
        out_specs=[IN_VMEM] * 8,
        out_shape=[
            pltpu.VMEM((slots, HD), jnp.float32),
            pltpu.VMEM(mask.shape, jnp.float32),
            pltpu.VMEM((1, gain.shape[0]), jnp.float32),
            pltpu.VMEM(hidden.shape, jnp.float32),
            *column_shapes(arrays, columns),
        ],
        scratch_shapes=[
            pltpu.SMEM(mem_len.shape, mem_len.dtype),
            *[pltpu.VMEM(x.shape, x.dtype) for x in small[1:]],
            pltpu.SemaphoreType.DMA((4,)),
            pltpu.SemaphoreType.DMA((8,)),
        ],
        compiler_params=small_vmem(2),
        name="setup",
    )(*in_hbm(small), *in_hbm(arrays))


def attention_kernel(groups, near_ref, far_ref, gain_ref, bias_ref, real_ref, *refs):
    loaded, refs = refs[: 4 * groups], refs[4 * groups :]
    sources, refs = refs[:4], refs[4:]
    send_ref, keep_ref, sg_ref, key_ref, value_ref, att_ref, kg_ref, vg_ref = refs[:8]
    late, sems = refs[8:12], refs[12]
    half = near_ref.shape[0]
    slots = 2 * half
    tokens, columns = sources[2].shape
    heads = columns // HD
    places = []
    blocks = [loaded[4 * i : 4 * i + 4] for i in range(groups)] + [late]
    for block in blocks:
        places += [(block, slice(at, at + WIDE)) for at in range(0, block[0].shape[1], WIDE)]
    late_pair = len(places) - late[0].shape[1] // WIDE
    copies = column_copies(late_pair * WIDE, sources, late, sems)
    for copy in copies:
        copy.start()
    hidden = jnp.concatenate([near_ref[...], far_ref[...]], axis=0).astype(jnp.float32)
    inverse_rms = lax.rsqrt(jnp.mean(hidden * hidden, axis=-1, keepdims=True) + 1e-05)
    memory = (hidden * inverse_rms * gain_ref[...]).astype(jnp.bfloat16)
    bias = jnp.concatenate([bias_ref[...]] * (CHUNK // HD), axis=1)
    real = real_ref[...]

    def project(pair):
        if pair == late_pair:
            for copy in copies:
                copy.wait()
        (kw_ref, vw_ref, _, _), at = places[pair]
        to = slice(pair * WIDE, (pair + 1) * WIDE)
        key_ref[:, to] = nn(memory, kw_ref[:, at]).astype(jnp.bfloat16)
        value_ref[:, to] = nn(memory, vw_ref[:, at]).astype(jnp.bfloat16)

    def parts(head):
        (_, _, q_ref, g_ref), at = places[head // 2]
        first = at.start + (head % 2) * HD
        return q_ref, g_ref, slice(first, first + HD)

    def softmax(head):
        at, here = slice(head * HD, (head + 1) * HD), slice(head * slots, (head + 1) * slots)
        q_ref, g_ref, own = parts(head)
        for chunk in range(tokens // CHUNK):
            part = slice(chunk * CHUNK, (chunk + 1) * CHUNK)
            scores = nt(key_ref[:, at], q_ref[part, own]) + bias
            grad_scores = nt(value_ref[:, at], g_ref[part, own])
            top = jnp.max(scores, axis=0, keepdims=True)
            exponent = jnp.exp2((scores - top) * (SCALE * LOG2E))
            attention = exponent * (real[:, part] / jnp.sum(exponent, axis=0, keepdims=True))
            delta = jnp.sum(attention * grad_scores, axis=0, keepdims=True)
            sg_ref[here, part] = (attention * (grad_scores - delta)).astype(jnp.bfloat16)
            att_ref[head % 4, :, part] = attention.astype(jnp.bfloat16)

    def product(head):
        at, here = slice(head * HD, (head + 1) * HD), slice(head * slots, (head + 1) * slots)
        q_ref, g_ref, own = parts(head)
        kg_ref[:, at] = (nn(sg_ref[here, :], q_ref[:, own]) * SCALE).astype(jnp.bfloat16)
        vg_ref[:, at] = nn(att_ref[head % 4], g_ref[:, own]).astype(jnp.bfloat16)

    project(0)
    for head in range(heads):
        if head % 2 == 0 and head + 2 < heads:
            project(head // 2 + 1)
        softmax(head)
        if head > 0:
            product(head - 1)
    product(heads - 1)
    key_weight = jnp.concatenate([block[0][...] for block in blocks], axis=1)
    value_weight = jnp.concatenate([block[1][...] for block in blocks], axis=1)
    partial = nt(kg_ref[...], key_weight) + nt(vg_ref[...], value_weight)
    keep_ref[...] = partial[:half]
    send_ref[...] = partial[half:].astype(jnp.bfloat16)


def attention_call(near, far, gain, bias, real, loaded, arrays):
    half, width = near.shape
    slots = 2 * half
    tokens, columns = arrays[2].shape
    heads = columns // HD
    late = columns - sum(x.shape[1] for x in loaded[::4])
    scratch = lambda *shape: pltpu.VMEM(shape, jnp.bfloat16)
    operands = [near, far, gain, bias, real, *loaded]
    return pl.pallas_call(
        functools.partial(attention_kernel, len(loaded) // 4),
        in_specs=[IN_VMEM] * len(operands) + [IN_HBM] * 4,
        out_specs=[IN_VMEM] * 4,
        out_shape=[
            pltpu.VMEM((half, width), jnp.bfloat16),
            pltpu.VMEM((half, width), jnp.float32),
            pltpu.VMEM((heads * slots, tokens), jnp.bfloat16),
            pltpu.VMEM((slots, columns), jnp.bfloat16),
        ],
        scratch_shapes=[
            scratch(slots, columns),
            scratch(4, slots, tokens),
            scratch(slots, columns),
            scratch(slots, columns),
            *column_shapes(arrays, late),
            pltpu.SemaphoreType.DMA((8,)),
        ],
        compiler_params=small_vmem(12 + 2 * slots * columns * 10 // 2**20),
        name="attention_backward",
    )(*[to_vmem(x) for x in operands], *in_hbm(arrays))


def query_kernel(first, heads, sg_ref, key_ref, *refs):
    out_ref, block_ref, sems = refs[-3:]
    slots = key_ref.shape[0]
    copies = []
    for index in range(heads):
        head = first + index
        at, here = slice(head * HD, (head + 1) * HD), slice(head * slots, (head + 1) * slots)
        block_ref[index] = (tn(sg_ref[here, :], key_ref[:, at]) * SCALE).astype(jnp.bfloat16)
        copies.append(pltpu.make_async_copy(block_ref.at[index], out_ref.at[:, at], sems.at[index]))
        copies[-1].start()
    for copy in copies:
        copy.wait()


def query_call(first, heads, score_grad, keys, so_far):
    columns = keys.shape[1]
    tokens = score_grad.shape[1]
    before = [] if so_far is None else [so_far]
    return pl.pallas_call(
        functools.partial(query_kernel, first, heads),
        in_specs=[IN_VMEM] * 2 + [pl.BlockSpec(memory_space=pl.ANY)] * len(before),
        out_specs=pl.BlockSpec(memory_space=pl.ANY),
        out_shape=jax.ShapeDtypeStruct((tokens, columns), jnp.bfloat16),
        scratch_shapes=[
            pltpu.VMEM((heads, tokens, HD), jnp.bfloat16),
            pltpu.SemaphoreType.DMA((heads,)),
        ],
        input_output_aliases={2: 0} if before else {},
        compiler_params=small_vmem(8),
        name="query_grad",
    )(to_vmem(score_grad), to_vmem(keys), *before)


def norm_kernel(own_ref, other_ref, hid_ref, gain_ref, out_ref):
    norm_grad = own_ref[...] + other_ref[...].astype(jnp.float32)
    hidden = hid_ref[...]
    inverse_rms = lax.rsqrt(jnp.mean(hidden * hidden, axis=-1, keepdims=True) + 1e-05)
    normed = hidden * inverse_rms
    scaled = norm_grad * gain_ref[...]
    inner_mean = jnp.mean(scaled * normed, axis=-1, keepdims=True)
    out_ref[...] = (inverse_rms * (scaled - normed * inner_mean)).astype(jnp.bfloat16)


def shards(size, queries, out_grad, query_mask, enc_hidden, norm_gain, key_weight, value_weight, mem_len):
    rows, width = enc_hidden.shape
    bits = size.bit_length() - 1
    heads = queries.shape[1] // HD
    arrays = (key_weight, value_weight, queries, out_grad)
    small = (mem_len, query_mask.reshape(1, -1), norm_gain, enc_hidden)
    early = [
        functools.partial(setup_call, rows, bits, size * rows, 0, WIDE, *small),
        functools.partial(load_call, WIDE, 2 * WIDE),
        functools.partial(load_call, 3 * WIDE, 2 * WIDE),
    ]
    ready = []
    near = enc_hidden
    for step in range(bits):
        far = exchange(near, size >> (step + 1), size)
        if step < len(early):
            given = lax.optimization_barrier((near, arrays))[1] if step else arrays
            far, made = lax.optimization_barrier((far, early[step](*given)))
            ready += made
        if step < bits - 1:
            near = lax.optimization_barrier(jnp.concatenate([near, far], axis=0))
    bias, real, gain, hidden, *loaded = ready
    send, keep, score_grad, keys = attention_call(near, far, gain, bias, real, loaded, arrays)
    query_grad = None
    shares = [(1, 0, 6), (2, 6, 5), (3, 11, 5)]
    for bit in range(bits):
        received = exchange(send, 1 << bit, size)
        for at, first, count in shares:
            if at == bit:
                score_grad, send = lax.optimization_barrier((score_grad, send))
                query_grad = query_call(first, count, score_grad, keys, query_grad)
                received, query_grad = lax.optimization_barrier((received, query_grad))
        if bit < bits - 1:
            half = keep.shape[0] // 2
            total = keep + received.astype(jnp.float32)
            keep, send = total[:half], total[half:].astype(jnp.bfloat16)
    operands = [keep, received, hidden, gain]
    hidden_grad = pl.pallas_call(
        norm_kernel,
        in_specs=[IN_VMEM] * 4,
        out_specs=IN_VMEM,
        out_shape=jax.ShapeDtypeStruct((rows, width), jnp.bfloat16),
        compiler_params=small_vmem(2),
        name="norm_backward",
    )(*[to_vmem(x) for x in operands])
    return (query_grad, hidden_grad)


def solution(mesh):
    in_specs = (
        P(("parts", "seq"), None),
        P(("parts", "seq"), None),
        P(("parts", "seq")),
        P(("parts", "seq"), None),
        P(),
        P(),
        P(),
        P("parts"),
    )
    out_specs = (P(("parts", "seq"), None), P(("parts", "seq"), None))
    body = functools.partial(shards, mesh.shape["seq"])
    return jax.shard_map(body, mesh=mesh, in_specs=in_specs, out_specs=out_specs, check_vma=False)
```

```python
import functools
import math

import jax
import jax.numpy as jnp
from jax import lax
from jax.experimental import pallas as pl
from jax.experimental.pallas import tpu as pltpu
from jax.sharding import PartitionSpec as P

HD = 128
CHUNK = 256
SCALE = 1.0 / math.sqrt(HD)
LOG2E = 1.4426950408889634
IN_VMEM = pl.BlockSpec(memory_space=pltpu.VMEM)
IN_HBM = pl.BlockSpec(memory_space=pltpu.HBM)
WIDE = 2 * HD


def exchange(array, distance, size):
    return lax.ppermute(array, "seq", [(i, i ^ distance) for i in range(size)])


def owner_offset(index, bits):
    offset = 0
    for bit in range(bits):
        offset |= ((index >> bit) & 1) << (bits - 1 - bit)
    return offset


def nt(a, b):
    return lax.dot_general(a, b, (((1,), (1,)), ((), ())), preferred_element_type=jnp.float32)


def nn(a, b):
    return lax.dot_general(a, b, (((1,), (0,)), ((), ())), preferred_element_type=jnp.float32)


def tn(a, b):
    return lax.dot_general(a, b, (((0,), (0,)), ((), ())), preferred_element_type=jnp.float32)


def small_vmem(mebibytes):
    return pltpu.CompilerParams(vmem_limit_bytes=mebibytes * 2**20)


def to_vmem(array):
    return pltpu.with_memory_space_constraint(array, pltpu.VMEM)


def column_copies(first, sources, targets, sems):
    copies = []
    for index, (source, target) in enumerate(zip(sources, targets)):
        rows, columns = target.shape
        for half in range(2):
            at = slice(half * rows // 2, (half + 1) * rows // 2)
            copies.append(
                pltpu.make_async_copy(
                    source.at[at, first : first + columns], target.at[at], sems.at[2 * index + half]
                )
            )
    return copies


def load_kernel(first, *refs):
    copies = column_copies(first, refs[:4], refs[4:8], refs[8])
    for copy in copies:
        copy.start()
    for copy in copies:
        copy.wait()


def in_hbm(arrays):
    return [pltpu.with_memory_space_constraint(x, pltpu.HBM) for x in arrays]


def column_shapes(arrays, columns):
    return [pltpu.VMEM((x.shape[0], columns), x.dtype) for x in arrays]


def load_call(first, columns, *arrays):
    return pl.pallas_call(
        functools.partial(load_kernel, first),
        in_specs=[IN_HBM] * 4,
        out_specs=[IN_VMEM] * 4,
        out_shape=column_shapes(arrays, columns),
        scratch_shapes=[pltpu.SemaphoreType.DMA((8,))],
        compiler_params=small_vmem(1),
        name="load",
    )(*in_hbm(arrays))


def setup_kernel(rows, bits, first, *refs):
    small, refs = refs[:4], refs[4:]
    sources, (bias_ref, real_ref, gain_out, hid_out), targets = refs[:4], refs[4:8], refs[8:12]
    held, small_sems, sems = refs[12:16], refs[16], refs[17]
    near = [pltpu.make_async_copy(small[i], held[i], small_sems.at[i]) for i in range(4)]
    copies = column_copies(first, sources, targets, sems)
    for copy in near + copies:
        copy.start()
    for copy in near:
        copy.wait()
    len_ref, mask_ref, gain_ref, hid_ref = held
    slots = bias_ref.shape[0]
    me = lax.axis_index("seq")
    row = lax.broadcasted_iota(jnp.int32, (slots, HD), 0)
    group = row // rows
    length = jnp.zeros((slots, HD), jnp.int32)
    for index in range(slots // rows):
        length = jnp.where(group == index, len_ref[me ^ owner_offset(index, bits)], length)
    bias_ref[...] = jnp.where(row - group * rows < length, 0.0, -jnp.inf)
    real_ref[...] = mask_ref[...].astype(jnp.float32)
    gain_out[...] = gain_ref[...].astype(jnp.float32).reshape(1, -1)
    hid_out[...] = hid_ref[...].astype(jnp.float32)
    for copy in copies:
        copy.wait()


def setup_call(rows, bits, slots, first, columns, mem_len, mask, gain, hidden, *arrays):
    small = (mem_len, mask, gain, hidden)
    return pl.pallas_call(
        functools.partial(setup_kernel, rows, bits, first),
        in_specs=[IN_HBM] * 8,
        out_specs=[IN_VMEM] * 8,
        out_shape=[
            pltpu.VMEM((slots, HD), jnp.float32),
            pltpu.VMEM(mask.shape, jnp.float32),
            pltpu.VMEM((1, gain.shape[0]), jnp.float32),
            pltpu.VMEM(hidden.shape, jnp.float32),
            *column_shapes(arrays, columns),
        ],
        scratch_shapes=[
            pltpu.SMEM(mem_len.shape, mem_len.dtype),
            *[pltpu.VMEM(x.shape, x.dtype) for x in small[1:]],
            pltpu.SemaphoreType.DMA((4,)),
            pltpu.SemaphoreType.DMA((8,)),
        ],
        compiler_params=small_vmem(2),
        name="setup",
    )(*in_hbm(small), *in_hbm(arrays))


def attention_kernel(groups, near_ref, far_ref, gain_ref, bias_ref, real_ref, *refs):
    loaded, refs = refs[: 4 * groups], refs[4 * groups :]
    send_ref, keep_ref, sg_ref, key_ref, value_ref, att_ref, kg_ref, vg_ref = refs
    half = near_ref.shape[0]
    slots = 2 * half
    tokens = loaded[2].shape[0]
    places = []
    blocks = [loaded[4 * i : 4 * i + 4] for i in range(groups)]
    for block in blocks:
        places += [(block, slice(at, at + WIDE)) for at in range(0, block[0].shape[1], WIDE)]
    heads = 2 * len(places)
    hidden = jnp.concatenate([near_ref[...], far_ref[...]], axis=0).astype(jnp.float32)
    inverse_rms = lax.rsqrt(jnp.mean(hidden * hidden, axis=-1, keepdims=True) + 1e-05)
    memory = (hidden * inverse_rms * gain_ref[...]).astype(jnp.bfloat16)
    bias = jnp.concatenate([bias_ref[...]] * (CHUNK // HD), axis=1)
    real = real_ref[...]

    def project(pair):
        (kw_ref, vw_ref, _, _), at = places[pair]
        to = slice(pair * WIDE, (pair + 1) * WIDE)
        key_ref[:, to] = nn(memory, kw_ref[:, at]).astype(jnp.bfloat16)
        value_ref[:, to] = nn(memory, vw_ref[:, at]).astype(jnp.bfloat16)

    def parts(head):
        (_, _, q_ref, g_ref), at = places[head // 2]
        first = at.start + (head % 2) * HD
        return q_ref, g_ref, slice(first, first + HD)

    def softmax(head):
        at, here = slice(head * HD, (head + 1) * HD), slice(head * slots, (head + 1) * slots)
        q_ref, g_ref, own = parts(head)
        for chunk in range(tokens // CHUNK):
            part = slice(chunk * CHUNK, (chunk + 1) * CHUNK)
            scores = nt(key_ref[:, at], q_ref[part, own]) + bias
            grad_scores = nt(value_ref[:, at], g_ref[part, own])
            top = jnp.max(scores, axis=0, keepdims=True)
            exponent = jnp.exp2((scores - top) * (SCALE * LOG2E))
            attention = exponent * (real[:, part] / jnp.sum(exponent, axis=0, keepdims=True))
            delta = jnp.sum(attention * grad_scores, axis=0, keepdims=True)
            sg_ref[here, part] = (attention * (grad_scores - delta)).astype(jnp.bfloat16)
            att_ref[head % 4, :, part] = attention.astype(jnp.bfloat16)

    def product(head):
        at, here = slice(head * HD, (head + 1) * HD), slice(head * slots, (head + 1) * slots)
        q_ref, g_ref, own = parts(head)
        kg_ref[:, at] = (nn(sg_ref[here, :], q_ref[:, own]) * SCALE).astype(jnp.bfloat16)
        vg_ref[:, at] = nn(att_ref[head % 4], g_ref[:, own]).astype(jnp.bfloat16)

    project(0)
    for head in range(heads):
        if head % 2 == 0 and head + 2 < heads:
            project(head // 2 + 1)
        softmax(head)
        if head > 0:
            product(head - 1)
    product(heads - 1)
    key_weight = jnp.concatenate([block[0][...] for block in blocks], axis=1)
    value_weight = jnp.concatenate([block[1][...] for block in blocks], axis=1)
    partial = nt(kg_ref[...], key_weight) + nt(vg_ref[...], value_weight)
    keep_ref[...] = partial[:half]
    send_ref[...] = partial[half:].astype(jnp.bfloat16)


def attention_call(near, far, gain, bias, real, loaded):
    half, width = near.shape
    slots = 2 * half
    tokens = loaded[2].shape[0]
    columns = sum(x.shape[1] for x in loaded[::4])
    heads = columns // HD
    scratch = lambda *shape: pltpu.VMEM(shape, jnp.bfloat16)
    operands = [near, far, gain, bias, real, *loaded]
    return pl.pallas_call(
        functools.partial(attention_kernel, len(loaded) // 4),
        in_specs=[IN_VMEM] * len(operands),
        out_specs=[IN_VMEM] * 4,
        out_shape=[
            pltpu.VMEM((half, width), jnp.bfloat16),
            pltpu.VMEM((half, width), jnp.float32),
            pltpu.VMEM((heads * slots, tokens), jnp.bfloat16),
            pltpu.VMEM((slots, columns), jnp.bfloat16),
        ],
        scratch_shapes=[
            scratch(slots, columns),
            scratch(4, slots, tokens),
            scratch(slots, columns),
            scratch(slots, columns),
        ],
        compiler_params=small_vmem(8 + 2 * slots * columns * 10 // 2**20),
        name="attention_backward",
    )(*[to_vmem(x) for x in operands])


def query_kernel(first, heads, sg_ref, key_ref, *refs):
    out_ref, block_ref, sems = refs[-3:]
    slots = key_ref.shape[0]
    copies = []
    for index in range(heads):
        head = first + index
        at, here = slice(head * HD, (head + 1) * HD), slice(head * slots, (head + 1) * slots)
        block_ref[index] = (tn(sg_ref[here, :], key_ref[:, at]) * SCALE).astype(jnp.bfloat16)
        copies.append(pltpu.make_async_copy(block_ref.at[index], out_ref.at[:, at], sems.at[index]))
        copies[-1].start()
    for copy in copies:
        copy.wait()


def query_call(first, heads, score_grad, keys, so_far):
    columns = keys.shape[1]
    tokens = score_grad.shape[1]
    before = [] if so_far is None else [so_far]
    return pl.pallas_call(
        functools.partial(query_kernel, first, heads),
        in_specs=[IN_VMEM] * 2 + [pl.BlockSpec(memory_space=pl.ANY)] * len(before),
        out_specs=pl.BlockSpec(memory_space=pl.ANY),
        out_shape=jax.ShapeDtypeStruct((tokens, columns), jnp.bfloat16),
        scratch_shapes=[
            pltpu.VMEM((heads, tokens, HD), jnp.bfloat16),
            pltpu.SemaphoreType.DMA((heads,)),
        ],
        input_output_aliases={2: 0} if before else {},
        compiler_params=small_vmem(8),
        name="query_grad",
    )(to_vmem(score_grad), to_vmem(keys), *before)


def norm_kernel(own_ref, other_ref, hid_ref, gain_ref, out_ref):
    norm_grad = own_ref[...] + other_ref[...].astype(jnp.float32)
    hidden = hid_ref[...]
    inverse_rms = lax.rsqrt(jnp.mean(hidden * hidden, axis=-1, keepdims=True) + 1e-05)
    normed = hidden * inverse_rms
    scaled = norm_grad * gain_ref[...]
    inner_mean = jnp.mean(scaled * normed, axis=-1, keepdims=True)
    out_ref[...] = (inverse_rms * (scaled - normed * inner_mean)).astype(jnp.bfloat16)


def shards(size, queries, out_grad, query_mask, enc_hidden, norm_gain, key_weight, value_weight, mem_len):
    rows, width = enc_hidden.shape
    bits = size.bit_length() - 1
    heads = queries.shape[1] // HD
    arrays = (key_weight, value_weight, queries, out_grad)
    small = (mem_len, query_mask.reshape(1, -1), norm_gain, enc_hidden)
    early = [
        functools.partial(setup_call, rows, bits, size * rows, 0, WIDE, *small),
        functools.partial(load_call, WIDE, 3 * WIDE),
        functools.partial(load_call, 4 * WIDE, 3 * WIDE),
        functools.partial(load_call, 7 * WIDE, queries.shape[1] - 7 * WIDE),
    ]
    ready = []
    near = enc_hidden
    for step in range(bits):
        far = exchange(near, size >> (step + 1), size)
        if step < len(early):
            given = lax.optimization_barrier((near, arrays))[1] if step else arrays
            far, made = lax.optimization_barrier((far, early[step](*given)))
            ready += made
        if step < bits - 1:
            near = lax.optimization_barrier(jnp.concatenate([near, far], axis=0))
    bias, real, gain, hidden, *loaded = ready
    send, keep, score_grad, keys = attention_call(near, far, gain, bias, real, loaded)
    query_grad = None
    shares = [(1, 0, 6), (2, 6, 5), (3, 11, 5)]
    for bit in range(bits):
        received = exchange(send, 1 << bit, size)
        for at, first, count in shares:
            if at == bit:
                score_grad, send = lax.optimization_barrier((score_grad, send))
                query_grad = query_call(first, count, score_grad, keys, query_grad)
                received, query_grad = lax.optimization_barrier((received, query_grad))
        if bit < bits - 1:
            half = keep.shape[0] // 2
            total = keep + received.astype(jnp.float32)
            keep, send = total[:half], total[half:].astype(jnp.bfloat16)
    operands = [keep, received, hidden, gain]
    hidden_grad = pl.pallas_call(
        norm_kernel,
        in_specs=[IN_VMEM] * 4,
        out_specs=IN_VMEM,
        out_shape=jax.ShapeDtypeStruct((rows, width), jnp.bfloat16),
        compiler_params=small_vmem(2),
        name="norm_backward",
    )(*[to_vmem(x) for x in operands])
    return (query_grad, hidden_grad)


def solution(mesh):
    in_specs = (
        P(("parts", "seq"), None),
        P(("parts", "seq"), None),
        P(("parts", "seq")),
        P(("parts", "seq"), None),
        P(),
        P(),
        P(),
        P("parts"),
    )
    out_specs = (P(("parts", "seq"), None), P(("parts", "seq"), None))
    body = functools.partial(shards, mesh.shape["seq"])
    return jax.shard_map(body, mesh=mesh, in_specs=in_specs, out_specs=out_specs, check_vma=False)
```

```python
import functools
import math

import jax
import jax.numpy as jnp
from jax import lax
from jax.experimental import pallas as pl
from jax.experimental.pallas import tpu as pltpu
from jax.sharding import PartitionSpec as P

HD = 128
CHUNK = 256
SCALE = 1.0 / math.sqrt(HD)
LOG2E = 1.4426950408889634
IN_VMEM = pl.BlockSpec(memory_space=pltpu.VMEM)
IN_HBM = pl.BlockSpec(memory_space=pltpu.HBM)
WIDE = 2 * HD


def exchange(array, distance, size):
    return lax.ppermute(array, "seq", [(i, i ^ distance) for i in range(size)])


def distances(size):
    far = [size >> (step + 1) for step in range(size.bit_length() - 2)]
    return [distance ^ 1 for distance in far] + [1]


def owner_offset(index, size):
    offset = 0
    for bit, distance in enumerate(distances(size)):
        if (index >> bit) & 1:
            offset ^= distance
    return offset


def nt(a, b):
    return lax.dot_general(a, b, (((1,), (1,)), ((), ())), preferred_element_type=jnp.float32)


def nn(a, b):
    return lax.dot_general(a, b, (((1,), (0,)), ((), ())), preferred_element_type=jnp.float32)


def tn(a, b):
    return lax.dot_general(a, b, (((0,), (0,)), ((), ())), preferred_element_type=jnp.float32)


def small_vmem(mebibytes):
    return pltpu.CompilerParams(vmem_limit_bytes=mebibytes * 2**20)


def to_vmem(array):
    return pltpu.with_memory_space_constraint(array, pltpu.VMEM)


def column_copies(first, sources, targets, sems):
    copies = []
    for index, (source, target) in enumerate(zip(sources, targets)):
        rows, columns = target.shape
        for half in range(2):
            at = slice(half * rows // 2, (half + 1) * rows // 2)
            copies.append(
                pltpu.make_async_copy(
                    source.at[at, first : first + columns], target.at[at], sems.at[2 * index + half]
                )
            )
    return copies


def load_kernel(first, *refs):
    copies = column_copies(first, refs[:4], refs[4:8], refs[8])
    for copy in copies:
        copy.start()
    for copy in copies:
        copy.wait()


def in_hbm(arrays):
    return [pltpu.with_memory_space_constraint(x, pltpu.HBM) for x in arrays]


def column_shapes(arrays, columns):
    return [pltpu.VMEM((x.shape[0], columns), x.dtype) for x in arrays]


def load_call(first, columns, *arrays):
    return pl.pallas_call(
        functools.partial(load_kernel, first),
        in_specs=[IN_HBM] * 4,
        out_specs=[IN_VMEM] * 4,
        out_shape=column_shapes(arrays, columns),
        scratch_shapes=[pltpu.SemaphoreType.DMA((8,))],
        compiler_params=small_vmem(1),
        name="load",
    )(*in_hbm(arrays))


def setup_kernel(rows, bits, first, *refs):
    small, refs = refs[:4], refs[4:]
    sources, (bias_ref, real_ref, gain_out, hid_out), targets = refs[:4], refs[4:8], refs[8:12]
    held, small_sems, sems = refs[12:16], refs[16], refs[17]
    near = [pltpu.make_async_copy(small[i], held[i], small_sems.at[i]) for i in range(4)]
    copies = column_copies(first, sources, targets, sems)
    for copy in near + copies:
        copy.start()
    for copy in near:
        copy.wait()
    len_ref, mask_ref, gain_ref, hid_ref = held
    slots = bias_ref.shape[0]
    me = lax.axis_index("seq")
    row = lax.broadcasted_iota(jnp.int32, (slots, HD), 0)
    group = row // rows
    length = jnp.zeros((slots, HD), jnp.int32)
    for index in range(slots // rows):
        length = jnp.where(group == index, len_ref[me ^ owner_offset(index, slots // rows)], length)
    bias_ref[...] = jnp.where(row - group * rows < length, 0.0, -jnp.inf)
    real_ref[...] = mask_ref[...].astype(jnp.float32)
    gain_out[...] = gain_ref[...].astype(jnp.float32).reshape(1, -1)
    hid_out[...] = hid_ref[...].astype(jnp.float32)
    for copy in copies:
        copy.wait()


def setup_call(rows, bits, slots, first, columns, mem_len, mask, gain, hidden, *arrays):
    small = (mem_len, mask, gain, hidden)
    return pl.pallas_call(
        functools.partial(setup_kernel, rows, bits, first),
        in_specs=[IN_HBM] * 8,
        out_specs=[IN_VMEM] * 8,
        out_shape=[
            pltpu.VMEM((slots, HD), jnp.float32),
            pltpu.VMEM(mask.shape, jnp.float32),
            pltpu.VMEM((1, gain.shape[0]), jnp.float32),
            pltpu.VMEM(hidden.shape, jnp.float32),
            *column_shapes(arrays, columns),
        ],
        scratch_shapes=[
            pltpu.SMEM(mem_len.shape, mem_len.dtype),
            *[pltpu.VMEM(x.shape, x.dtype) for x in small[1:]],
            pltpu.SemaphoreType.DMA((4,)),
            pltpu.SemaphoreType.DMA((8,)),
        ],
        compiler_params=small_vmem(2),
        name="setup",
    )(*in_hbm(small), *in_hbm(arrays))


def attention_kernel(groups, near_ref, far_ref, gain_ref, bias_ref, real_ref, *refs):
    loaded, refs = refs[: 4 * groups], refs[4 * groups :]
    send_ref, keep_ref, sg_ref, key_ref, value_ref, att_ref, kg_ref, vg_ref = refs
    half = near_ref.shape[0]
    slots = 2 * half
    tokens = loaded[2].shape[0]
    places = []
    blocks = [loaded[4 * i : 4 * i + 4] for i in range(groups)]
    for block in blocks:
        places += [(block, slice(at, at + WIDE)) for at in range(0, block[0].shape[1], WIDE)]
    heads = 2 * len(places)
    hidden = jnp.concatenate([near_ref[...], far_ref[...]], axis=0).astype(jnp.float32)
    inverse_rms = lax.rsqrt(jnp.mean(hidden * hidden, axis=-1, keepdims=True) + 1e-05)
    memory = (hidden * inverse_rms * gain_ref[...]).astype(jnp.bfloat16)
    bias = jnp.concatenate([bias_ref[...]] * (CHUNK // HD), axis=1)
    real = real_ref[...]

    def project(pair):
        (kw_ref, vw_ref, _, _), at = places[pair]
        to = slice(pair * WIDE, (pair + 1) * WIDE)
        key_ref[:, to] = nn(memory, kw_ref[:, at]).astype(jnp.bfloat16)
        value_ref[:, to] = nn(memory, vw_ref[:, at]).astype(jnp.bfloat16)

    def parts(head):
        (_, _, q_ref, g_ref), at = places[head // 2]
        first = at.start + (head % 2) * HD
        return q_ref, g_ref, slice(first, first + HD)

    def softmax(head):
        at, here = slice(head * HD, (head + 1) * HD), slice(head * slots, (head + 1) * slots)
        q_ref, g_ref, own = parts(head)
        for chunk in range(tokens // CHUNK):
            part = slice(chunk * CHUNK, (chunk + 1) * CHUNK)
            scores = nt(key_ref[:, at], q_ref[part, own]) + bias
            grad_scores = nt(value_ref[:, at], g_ref[part, own])
            top = jnp.max(scores, axis=0, keepdims=True)
            exponent = jnp.exp2((scores - top) * (SCALE * LOG2E))
            attention = exponent * (real[:, part] / jnp.sum(exponent, axis=0, keepdims=True))
            delta = jnp.sum(attention * grad_scores, axis=0, keepdims=True)
            sg_ref[here, part] = (attention * (grad_scores - delta)).astype(jnp.bfloat16)
            att_ref[head % 4, :, part] = attention.astype(jnp.bfloat16)

    def product(head):
        at, here = slice(head * HD, (head + 1) * HD), slice(head * slots, (head + 1) * slots)
        q_ref, g_ref, own = parts(head)
        kg_ref[:, at] = (nn(sg_ref[here, :], q_ref[:, own]) * SCALE).astype(jnp.bfloat16)
        vg_ref[:, at] = nn(att_ref[head % 4], g_ref[:, own]).astype(jnp.bfloat16)

    project(0)
    for head in range(heads):
        if head % 2 == 0 and head + 2 < heads:
            project(head // 2 + 1)
        softmax(head)
        if head > 0:
            product(head - 1)
    product(heads - 1)
    key_weight = jnp.concatenate([block[0][...] for block in blocks], axis=1)
    value_weight = jnp.concatenate([block[1][...] for block in blocks], axis=1)
    partial = nt(kg_ref[...], key_weight) + nt(vg_ref[...], value_weight)
    keep_ref[...] = partial[:half]
    send_ref[...] = partial[half:].astype(jnp.bfloat16)


def attention_call(near, far, gain, bias, real, loaded):
    half, width = near.shape
    slots = 2 * half
    tokens = loaded[2].shape[0]
    columns = sum(x.shape[1] for x in loaded[::4])
    heads = columns // HD
    scratch = lambda *shape: pltpu.VMEM(shape, jnp.bfloat16)
    operands = [near, far, gain, bias, real, *loaded]
    return pl.pallas_call(
        functools.partial(attention_kernel, len(loaded) // 4),
        in_specs=[IN_VMEM] * len(operands),
        out_specs=[IN_VMEM] * 4,
        out_shape=[
            pltpu.VMEM((half, width), jnp.bfloat16),
            pltpu.VMEM((half, width), jnp.float32),
            pltpu.VMEM((heads * slots, tokens), jnp.bfloat16),
            pltpu.VMEM((slots, columns), jnp.bfloat16),
        ],
        scratch_shapes=[
            scratch(slots, columns),
            scratch(4, slots, tokens),
            scratch(slots, columns),
            scratch(slots, columns),
        ],
        compiler_params=small_vmem(8 + 2 * slots * columns * 10 // 2**20),
        name="attention_backward",
    )(*[to_vmem(x) for x in operands])


def query_kernel(first, heads, sg_ref, key_ref, *refs):
    out_ref, block_ref, sems = refs[-3:]
    slots = key_ref.shape[0]
    copies = []
    for index in range(heads):
        head = first + index
        at, here = slice(head * HD, (head + 1) * HD), slice(head * slots, (head + 1) * slots)
        block_ref[index] = (tn(sg_ref[here, :], key_ref[:, at]) * SCALE).astype(jnp.bfloat16)
        copies.append(pltpu.make_async_copy(block_ref.at[index], out_ref.at[:, at], sems.at[index]))
        copies[-1].start()
    for copy in copies:
        copy.wait()


def query_call(first, heads, score_grad, keys, so_far):
    columns = keys.shape[1]
    tokens = score_grad.shape[1]
    before = [] if so_far is None else [so_far]
    return pl.pallas_call(
        functools.partial(query_kernel, first, heads),
        in_specs=[IN_VMEM] * 2 + [pl.BlockSpec(memory_space=pl.ANY)] * len(before),
        out_specs=pl.BlockSpec(memory_space=pl.ANY),
        out_shape=jax.ShapeDtypeStruct((tokens, columns), jnp.bfloat16),
        scratch_shapes=[
            pltpu.VMEM((heads, tokens, HD), jnp.bfloat16),
            pltpu.SemaphoreType.DMA((heads,)),
        ],
        input_output_aliases={2: 0} if before else {},
        compiler_params=small_vmem(8),
        name="query_grad",
    )(to_vmem(score_grad), to_vmem(keys), *before)


def norm_kernel(own_ref, other_ref, hid_ref, gain_ref, out_ref):
    norm_grad = own_ref[...] + other_ref[...].astype(jnp.float32)
    hidden = hid_ref[...]
    inverse_rms = lax.rsqrt(jnp.mean(hidden * hidden, axis=-1, keepdims=True) + 1e-05)
    normed = hidden * inverse_rms
    scaled = norm_grad * gain_ref[...]
    inner_mean = jnp.mean(scaled * normed, axis=-1, keepdims=True)
    out_ref[...] = (inverse_rms * (scaled - normed * inner_mean)).astype(jnp.bfloat16)


def shards(size, queries, out_grad, query_mask, enc_hidden, norm_gain, key_weight, value_weight, mem_len):
    rows, width = enc_hidden.shape
    bits = size.bit_length() - 1
    heads = queries.shape[1] // HD
    arrays = (key_weight, value_weight, queries, out_grad)
    small = (mem_len, query_mask.reshape(1, -1), norm_gain, enc_hidden)
    early = [
        functools.partial(setup_call, rows, bits, size * rows, 0, WIDE, *small),
        functools.partial(load_call, WIDE, 3 * WIDE),
        functools.partial(load_call, 4 * WIDE, 3 * WIDE),
        functools.partial(load_call, 7 * WIDE, queries.shape[1] - 7 * WIDE),
    ]
    ready = []
    near = enc_hidden
    for step in range(bits):
        far = exchange(near, distances(size)[step], size)
        if step < len(early):
            given = lax.optimization_barrier((near, arrays))[1] if step else arrays
            far, made = lax.optimization_barrier((far, early[step](*given)))
            ready += made
        if step < bits - 1:
            near = lax.optimization_barrier(jnp.concatenate([near, far], axis=0))
    bias, real, gain, hidden, *loaded = ready
    send, keep, score_grad, keys = attention_call(near, far, gain, bias, real, loaded)
    query_grad = None
    shares = [(1, 0, 6), (2, 6, 5), (3, 11, 5)]
    for bit in range(bits):
        received = exchange(send, distances(size)[bits - 1 - bit], size)
        for at, first, count in shares:
            if at == bit:
                score_grad, send = lax.optimization_barrier((score_grad, send))
                query_grad = query_call(first, count, score_grad, keys, query_grad)
                received, query_grad = lax.optimization_barrier((received, query_grad))
        if bit < bits - 1:
            half = keep.shape[0] // 2
            total = keep + received.astype(jnp.float32)
            keep, send = total[:half], total[half:].astype(jnp.bfloat16)
    operands = [keep, received, hidden, gain]
    hidden_grad = pl.pallas_call(
        norm_kernel,
        in_specs=[IN_VMEM] * 4,
        out_specs=IN_VMEM,
        out_shape=jax.ShapeDtypeStruct((rows, width), jnp.bfloat16),
        compiler_params=small_vmem(2),
        name="norm_backward",
    )(*[to_vmem(x) for x in operands])
    return (query_grad, hidden_grad)


def solution(mesh):
    in_specs = (
        P(("parts", "seq"), None),
        P(("parts", "seq"), None),
        P(("parts", "seq")),
        P(("parts", "seq"), None),
        P(),
        P(),
        P(),
        P("parts"),
    )
    out_specs = (P(("parts", "seq"), None), P(("parts", "seq"), None))
    body = functools.partial(shards, mesh.shape["seq"])
    return jax.shard_map(body, mesh=mesh, in_specs=in_specs, out_specs=out_specs, check_vma=False)
```

```python
import functools
import math

import jax
import jax.numpy as jnp
from jax import lax
from jax.experimental import pallas as pl
from jax.experimental.pallas import tpu as pltpu
from jax.sharding import PartitionSpec as P

HD = 128
CHUNK = 256
SCALE = 1.0 / math.sqrt(HD)
LOG2E = 1.4426950408889634
IN_VMEM = pl.BlockSpec(memory_space=pltpu.VMEM)
IN_HBM = pl.BlockSpec(memory_space=pltpu.HBM)
WIDE = 2 * HD


def exchange(array, distance, size):
    return lax.ppermute(array, "seq", [(i, i ^ distance) for i in range(size)])


def distances(size):
    far = [size >> (step + 1) for step in range(size.bit_length() - 2)]
    return [distance ^ 1 for distance in far] + [1]


def owner_offset(index, size):
    offset = 0
    for bit, distance in enumerate(distances(size)):
        if (index >> bit) & 1:
            offset ^= distance
    return offset


def nt(a, b):
    return lax.dot_general(a, b, (((1,), (1,)), ((), ())), preferred_element_type=jnp.float32)


def nn(a, b):
    return lax.dot_general(a, b, (((1,), (0,)), ((), ())), preferred_element_type=jnp.float32)


def tn(a, b):
    return lax.dot_general(a, b, (((0,), (0,)), ((), ())), preferred_element_type=jnp.float32)


def small_vmem(mebibytes):
    return pltpu.CompilerParams(vmem_limit_bytes=mebibytes * 2**20)


def to_vmem(array):
    return pltpu.with_memory_space_constraint(array, pltpu.VMEM)


def column_copies(first, sources, targets, sems):
    copies = []
    for index, (source, target) in enumerate(zip(sources, targets)):
        rows, columns = target.shape
        for half in range(2):
            at = slice(half * rows // 2, (half + 1) * rows // 2)
            copies.append(
                pltpu.make_async_copy(
                    source.at[at, first : first + columns], target.at[at], sems.at[2 * index + half]
                )
            )
    return copies


def load_kernel(first, *refs):
    copies = column_copies(first, refs[:4], refs[4:8], refs[8])
    for copy in copies:
        copy.start()
    for copy in copies:
        copy.wait()


def in_hbm(arrays):
    return [pltpu.with_memory_space_constraint(x, pltpu.HBM) for x in arrays]


def column_shapes(arrays, columns):
    return [pltpu.VMEM((x.shape[0], columns), x.dtype) for x in arrays]


def load_call(first, columns, *arrays):
    return pl.pallas_call(
        functools.partial(load_kernel, first),
        in_specs=[IN_HBM] * 4,
        out_specs=[IN_VMEM] * 4,
        out_shape=column_shapes(arrays, columns),
        scratch_shapes=[pltpu.SemaphoreType.DMA((8,))],
        compiler_params=small_vmem(1),
        name="load",
    )(*in_hbm(arrays))


def setup_kernel(rows, bits, first, *refs):
    small, refs = refs[:4], refs[4:]
    sources, (bias_ref, real_ref, gain_out, hid_out), targets = refs[:4], refs[4:8], refs[8:12]
    held, small_sems, sems = refs[12:16], refs[16], refs[17]
    near = [pltpu.make_async_copy(small[i], held[i], small_sems.at[i]) for i in range(4)]
    copies = column_copies(first, sources, targets, sems)
    for copy in near + copies:
        copy.start()
    for copy in near:
        copy.wait()
    len_ref, mask_ref, gain_ref, hid_ref = held
    slots = bias_ref.shape[0]
    me = lax.axis_index("seq")
    row = lax.broadcasted_iota(jnp.int32, (slots, HD), 0)
    group = row // rows
    length = jnp.zeros((slots, HD), jnp.int32)
    for index in range(slots // rows):
        length = jnp.where(group == index, len_ref[me ^ owner_offset(index, slots // rows)], length)
    bias_ref[...] = jnp.where(row - group * rows < length, 0.0, -jnp.inf)
    real_ref[...] = mask_ref[...].astype(jnp.float32)
    gain_out[...] = gain_ref[...].astype(jnp.float32).reshape(1, -1)
    hid_out[...] = hid_ref[...].astype(jnp.float32)
    for copy in copies:
        copy.wait()


def setup_call(rows, bits, slots, first, columns, mem_len, mask, gain, hidden, *arrays):
    small = (mem_len, mask, gain, hidden)
    return pl.pallas_call(
        functools.partial(setup_kernel, rows, bits, first),
        in_specs=[IN_HBM] * 8,
        out_specs=[IN_VMEM] * 8,
        out_shape=[
            pltpu.VMEM((slots, HD), jnp.float32),
            pltpu.VMEM(mask.shape, jnp.float32),
            pltpu.VMEM((1, gain.shape[0]), jnp.float32),
            pltpu.VMEM(hidden.shape, jnp.float32),
            *column_shapes(arrays, columns),
        ],
        scratch_shapes=[
            pltpu.SMEM(mem_len.shape, mem_len.dtype),
            *[pltpu.VMEM(x.shape, x.dtype) for x in small[1:]],
            pltpu.SemaphoreType.DMA((4,)),
            pltpu.SemaphoreType.DMA((8,)),
        ],
        compiler_params=small_vmem(2),
        name="setup",
    )(*in_hbm(small), *in_hbm(arrays))


def attention_kernel(groups, near_ref, far_ref, gain_ref, bias_ref, real_ref, *refs):
    loaded, refs = refs[: 4 * groups], refs[4 * groups :]
    send_ref, keep_ref, sg_ref, key_ref, value_ref, att_ref, kg_ref, vg_ref = refs
    half = near_ref.shape[0]
    slots = 2 * half
    tokens = loaded[2].shape[0]
    places = []
    blocks = [loaded[4 * i : 4 * i + 4] for i in range(groups)]
    for block in blocks:
        places += [(block, slice(at, at + WIDE)) for at in range(0, block[0].shape[1], WIDE)]
    heads = 2 * len(places)
    hidden = jnp.concatenate([near_ref[...], far_ref[...]], axis=0).astype(jnp.float32)
    inverse_rms = lax.rsqrt(jnp.mean(hidden * hidden, axis=-1, keepdims=True) + 1e-05)
    memory = (hidden * inverse_rms * gain_ref[...]).astype(jnp.bfloat16)
    bias = jnp.concatenate([bias_ref[...]] * (CHUNK // HD), axis=1)
    real = real_ref[...]

    def project(pair):
        (kw_ref, vw_ref, _, _), at = places[pair]
        to = slice(pair * WIDE, (pair + 1) * WIDE)
        key_ref[:, to] = nn(memory, kw_ref[:, at]).astype(jnp.bfloat16)
        value_ref[:, to] = nn(memory, vw_ref[:, at]).astype(jnp.bfloat16)

    def parts(head):
        (_, _, q_ref, g_ref), at = places[head // 2]
        first = at.start + (head % 2) * HD
        return q_ref, g_ref, slice(first, first + HD)

    def softmax(head):
        at, here = slice(head * HD, (head + 1) * HD), slice(head * slots, (head + 1) * slots)
        q_ref, g_ref, own = parts(head)
        for chunk in range(tokens // CHUNK):
            part = slice(chunk * CHUNK, (chunk + 1) * CHUNK)
            scores = nt(key_ref[:, at], q_ref[part, own]) + bias
            grad_scores = nt(value_ref[:, at], g_ref[part, own])
            top = jnp.max(scores, axis=0, keepdims=True)
            exponent = jnp.exp2((scores - top) * (SCALE * LOG2E))
            attention = exponent * (real[:, part] / jnp.sum(exponent, axis=0, keepdims=True))
            delta = jnp.sum(attention * grad_scores, axis=0, keepdims=True)
            sg_ref[here, part] = (attention * (grad_scores - delta)).astype(jnp.bfloat16)
            att_ref[head % 4, :, part] = attention.astype(jnp.bfloat16)

    def product(head):
        at, here = slice(head * HD, (head + 1) * HD), slice(head * slots, (head + 1) * slots)
        q_ref, g_ref, own = parts(head)
        kg_ref[:, at] = (nn(sg_ref[here, :], q_ref[:, own]) * SCALE).astype(jnp.bfloat16)
        vg_ref[:, at] = nn(att_ref[head % 4], g_ref[:, own]).astype(jnp.bfloat16)

    project(0)
    for head in range(heads):
        if head % 2 == 0 and head + 2 < heads:
            project(head // 2 + 1)
        softmax(head)
        if head > 0:
            product(head - 1)
    product(heads - 1)
    key_weight = jnp.concatenate([block[0][...] for block in blocks], axis=1)
    value_weight = jnp.concatenate([block[1][...] for block in blocks], axis=1)
    partial = nt(kg_ref[...], key_weight) + nt(vg_ref[...], value_weight)
    keep_ref[...] = partial[:half]
    send_ref[...] = partial[half:].astype(jnp.bfloat16)


def attention_call(near, far, gain, bias, real, loaded):
    half, width = near.shape
    slots = 2 * half
    tokens = loaded[2].shape[0]
    columns = sum(x.shape[1] for x in loaded[::4])
    heads = columns // HD
    scratch = lambda *shape: pltpu.VMEM(shape, jnp.bfloat16)
    operands = [near, far, gain, bias, real, *loaded]
    return pl.pallas_call(
        functools.partial(attention_kernel, len(loaded) // 4),
        in_specs=[IN_VMEM] * len(operands),
        out_specs=[IN_VMEM] * 4,
        out_shape=[
            pltpu.VMEM((half, width), jnp.bfloat16),
            pltpu.VMEM((half, width), jnp.float32),
            pltpu.VMEM((heads * slots, tokens), jnp.bfloat16),
            pltpu.VMEM((slots, columns), jnp.bfloat16),
        ],
        scratch_shapes=[
            scratch(slots, columns),
            scratch(4, slots, tokens),
            scratch(slots, columns),
            scratch(slots, columns),
        ],
        compiler_params=small_vmem(8 + 2 * slots * columns * 10 // 2**20),
        name="attention_backward",
    )(*[to_vmem(x) for x in operands])


def query_kernel(first, heads, sg_ref, key_ref, *refs):
    out_ref, block_ref, sems = refs[-3:]
    slots = key_ref.shape[0]
    copies = []
    for index in range(heads):
        head = first + index
        at, here = slice(head * HD, (head + 1) * HD), slice(head * slots, (head + 1) * slots)
        block_ref[index] = (tn(sg_ref[here, :], key_ref[:, at]) * SCALE).astype(jnp.bfloat16)
        copies.append(pltpu.make_async_copy(block_ref.at[index], out_ref.at[:, at], sems.at[index]))
        copies[-1].start()
    for copy in copies:
        copy.wait()


def query_call(first, heads, score_grad, keys, so_far):
    columns = keys.shape[1]
    tokens = score_grad.shape[1]
    before = [] if so_far is None else [so_far]
    return pl.pallas_call(
        functools.partial(query_kernel, first, heads),
        in_specs=[IN_VMEM] * 2 + [pl.BlockSpec(memory_space=pl.ANY)] * len(before),
        out_specs=pl.BlockSpec(memory_space=pl.ANY),
        out_shape=jax.ShapeDtypeStruct((tokens, columns), jnp.bfloat16),
        scratch_shapes=[
            pltpu.VMEM((heads, tokens, HD), jnp.bfloat16),
            pltpu.SemaphoreType.DMA((heads,)),
        ],
        input_output_aliases={2: 0} if before else {},
        compiler_params=small_vmem(8),
        name="query_grad",
    )(to_vmem(score_grad), to_vmem(keys), *before)


def norm_kernel(own_ref, other_ref, hid_ref, gain_ref, out_ref):
    norm_grad = own_ref[...] + other_ref[...].astype(jnp.float32)
    hidden = hid_ref[...]
    inverse_rms = lax.rsqrt(jnp.mean(hidden * hidden, axis=-1, keepdims=True) + 1e-05)
    normed = hidden * inverse_rms
    scaled = norm_grad * gain_ref[...]
    inner_mean = jnp.mean(scaled * normed, axis=-1, keepdims=True)
    out_ref[...] = (inverse_rms * (scaled - normed * inner_mean)).astype(jnp.bfloat16)


def shards(size, queries, out_grad, query_mask, enc_hidden, norm_gain, key_weight, value_weight, mem_len):
    rows, width = enc_hidden.shape
    bits = size.bit_length() - 1
    heads = queries.shape[1] // HD
    arrays = (key_weight, value_weight, queries, out_grad)
    small = (mem_len, query_mask.reshape(1, -1), norm_gain, enc_hidden)
    early = [
        functools.partial(setup_call, rows, bits, size * rows, 0, WIDE, *small),
        functools.partial(load_call, 1 * WIDE, 3 * WIDE),
        functools.partial(load_call, 4 * WIDE, queries.shape[1] - 4 * WIDE),
    ]
    ready = []
    near = enc_hidden
    for step in range(bits - 1):
        last = step == bits - 2
        far = exchange(near, distances(size)[step], size)
        others = [exchange(near, d ^ distances(size)[bits - 1], size) for d in (0, distances(size)[step])] if last else []
        if step < len(early):
            given = lax.optimization_barrier((near, arrays))[1] if step else arrays
            far, others, made = lax.optimization_barrier((far, others, early[step](*given)))
            ready += made
        near = lax.optimization_barrier(jnp.concatenate([near, far], axis=0))
    far = lax.optimization_barrier(jnp.concatenate(others, axis=0))
    bias, real, gain, hidden, *loaded = ready
    send, keep, score_grad, keys = attention_call(near, far, gain, bias, real, loaded)
    query_grad = None
    shares = [(1, 0, 6), (2, 6, 5), (3, 11, 5)]
    for bit in range(bits):
        received = exchange(send, distances(size)[bits - 1 - bit], size)
        for at, first, count in shares:
            if at == bit:
                score_grad, send = lax.optimization_barrier((score_grad, send))
                query_grad = query_call(first, count, score_grad, keys, query_grad)
                received, query_grad = lax.optimization_barrier((received, query_grad))
        if bit < bits - 1:
            half = keep.shape[0] // 2
            total = keep + received.astype(jnp.float32)
            keep, send = total[:half], total[half:].astype(jnp.bfloat16)
    operands = [keep, received, hidden, gain]
    hidden_grad = pl.pallas_call(
        norm_kernel,
        in_specs=[IN_VMEM] * 4,
        out_specs=IN_VMEM,
        out_shape=jax.ShapeDtypeStruct((rows, width), jnp.bfloat16),
        compiler_params=small_vmem(2),
        name="norm_backward",
    )(*[to_vmem(x) for x in operands])
    return (query_grad, hidden_grad)


def solution(mesh):
    in_specs = (
        P(("parts", "seq"), None),
        P(("parts", "seq"), None),
        P(("parts", "seq")),
        P(("parts", "seq"), None),
        P(),
        P(),
        P(),
        P("parts"),
    )
    out_specs = (P(("parts", "seq"), None), P(("parts", "seq"), None))
    body = functools.partial(shards, mesh.shape["seq"])
    return jax.shard_map(body, mesh=mesh, in_specs=in_specs, out_specs=out_specs, check_vma=False)
```

```python
import functools
import math

import jax
import jax.numpy as jnp
from jax import lax
from jax.experimental import pallas as pl
from jax.experimental.pallas import tpu as pltpu
from jax.sharding import PartitionSpec as P

HD = 128
CHUNK = 256
SCALE = 1.0 / math.sqrt(HD)
LOG2E = 1.4426950408889634
IN_VMEM = pl.BlockSpec(memory_space=pltpu.VMEM)
IN_HBM = pl.BlockSpec(memory_space=pltpu.HBM)
WIDE = 2 * HD


def exchange(array, distance, size):
    return lax.ppermute(array, "seq", [(i, i ^ distance) for i in range(size)])


def distances(size):
    far = [size >> (step + 1) for step in range(size.bit_length() - 2)]
    return [distance ^ 1 for distance in far] + [1]


def owner_offset(index, size):
    offset = 0
    for bit, distance in enumerate(distances(size)):
        if (index >> bit) & 1:
            offset ^= distance
    return offset


def nt(a, b):
    return lax.dot_general(a, b, (((1,), (1,)), ((), ())), preferred_element_type=jnp.float32)


def nn(a, b):
    return lax.dot_general(a, b, (((1,), (0,)), ((), ())), preferred_element_type=jnp.float32)


def tn(a, b):
    return lax.dot_general(a, b, (((0,), (0,)), ((), ())), preferred_element_type=jnp.float32)


def small_vmem(mebibytes):
    return pltpu.CompilerParams(vmem_limit_bytes=mebibytes * 2**20)


def to_vmem(array):
    return pltpu.with_memory_space_constraint(array, pltpu.VMEM)


def column_copies(first, sources, targets, sems):
    copies = []
    for index, (source, target) in enumerate(zip(sources, targets)):
        rows, columns = target.shape
        for half in range(2):
            at = slice(half * rows // 2, (half + 1) * rows // 2)
            copies.append(
                pltpu.make_async_copy(
                    source.at[at, first : first + columns], target.at[at], sems.at[2 * index + half]
                )
            )
    return copies


def load_kernel(first, *refs):
    copies = column_copies(first, refs[:4], refs[4:8], refs[8])
    for copy in copies:
        copy.start()
    for copy in copies:
        copy.wait()


def in_hbm(arrays):
    return [pltpu.with_memory_space_constraint(x, pltpu.HBM) for x in arrays]


def column_shapes(arrays, columns):
    return [pltpu.VMEM((x.shape[0], columns), x.dtype) for x in arrays]


def load_call(first, columns, *arrays):
    return pl.pallas_call(
        functools.partial(load_kernel, first),
        in_specs=[IN_HBM] * 4,
        out_specs=[IN_VMEM] * 4,
        out_shape=column_shapes(arrays, columns),
        scratch_shapes=[pltpu.SemaphoreType.DMA((8,))],
        compiler_params=small_vmem(1),
        name="load",
    )(*in_hbm(arrays))


def setup_kernel(rows, bits, first, *refs):
    small, refs = refs[:4], refs[4:]
    sources, (bias_ref, real_ref, gain_out, hid_out), targets = refs[:4], refs[4:8], refs[8:12]
    held, small_sems, sems = refs[12:16], refs[16], refs[17]
    near = [pltpu.make_async_copy(small[i], held[i], small_sems.at[i]) for i in range(4)]
    copies = column_copies(first, sources, targets, sems)
    for copy in near + copies:
        copy.start()
    for copy in near:
        copy.wait()
    len_ref, mask_ref, gain_ref, hid_ref = held
    slots = bias_ref.shape[0]
    me = lax.axis_index("seq")
    row = lax.broadcasted_iota(jnp.int32, (slots, HD), 0)
    group = row // rows
    length = jnp.zeros((slots, HD), jnp.int32)
    for index in range(slots // rows):
        length = jnp.where(group == index, len_ref[me ^ owner_offset(index, slots // rows)], length)
    bias_ref[...] = jnp.where(row - group * rows < length, 0.0, -jnp.inf)
    real_ref[...] = mask_ref[...].astype(jnp.float32)
    gain_out[...] = gain_ref[...].astype(jnp.float32).reshape(1, -1)
    hidden = hid_ref[...].astype(jnp.float32)
    inverse_rms = lax.rsqrt(jnp.mean(hidden * hidden, axis=-1, keepdims=True) + 1e-05)
    hid_out[0] = hidden * inverse_rms
    hid_out[1] = jnp.broadcast_to(inverse_rms, hidden.shape)
    for copy in copies:
        copy.wait()


def setup_call(rows, bits, slots, first, columns, mem_len, mask, gain, hidden, *arrays):
    small = (mem_len, mask, gain, hidden)
    return pl.pallas_call(
        functools.partial(setup_kernel, rows, bits, first),
        in_specs=[IN_HBM] * 8,
        out_specs=[IN_VMEM] * 8,
        out_shape=[
            pltpu.VMEM((slots, HD), jnp.float32),
            pltpu.VMEM(mask.shape, jnp.float32),
            pltpu.VMEM((1, gain.shape[0]), jnp.float32),
            pltpu.VMEM((2, *hidden.shape), jnp.float32),
            *column_shapes(arrays, columns),
        ],
        scratch_shapes=[
            pltpu.SMEM(mem_len.shape, mem_len.dtype),
            *[pltpu.VMEM(x.shape, x.dtype) for x in small[1:]],
            pltpu.SemaphoreType.DMA((4,)),
            pltpu.SemaphoreType.DMA((8,)),
        ],
        compiler_params=small_vmem(2),
        name="setup",
    )(*in_hbm(small), *in_hbm(arrays))


def attention_kernel(groups, near_ref, far_ref, gain_ref, bias_ref, real_ref, *refs):
    loaded, refs = refs[: 4 * groups], refs[4 * groups :]
    send_ref, keep_ref, sg_ref, key_ref, value_ref, att_ref, kg_ref, vg_ref = refs
    half = near_ref.shape[0]
    slots = 2 * half
    tokens = loaded[2].shape[0]
    places = []
    blocks = [loaded[4 * i : 4 * i + 4] for i in range(groups)]
    for block in blocks:
        places += [(block, slice(at, at + WIDE)) for at in range(0, block[0].shape[1], WIDE)]
    heads = 2 * len(places)
    hidden = jnp.concatenate([near_ref[...], far_ref[...]], axis=0).astype(jnp.float32)
    inverse_rms = lax.rsqrt(jnp.mean(hidden * hidden, axis=-1, keepdims=True) + 1e-05)
    memory = (hidden * inverse_rms * gain_ref[...]).astype(jnp.bfloat16)
    bias = jnp.concatenate([bias_ref[...]] * (CHUNK // HD), axis=1)
    real = real_ref[...]

    def project(pair):
        (kw_ref, vw_ref, _, _), at = places[pair]
        to = slice(pair * WIDE, (pair + 1) * WIDE)
        key_ref[:, to] = nn(memory, kw_ref[:, at]).astype(jnp.bfloat16)
        value_ref[:, to] = nn(memory, vw_ref[:, at]).astype(jnp.bfloat16)

    def parts(head):
        (_, _, q_ref, g_ref), at = places[head // 2]
        first = at.start + (head % 2) * HD
        return q_ref, g_ref, slice(first, first + HD)

    def softmax(head):
        at, here = slice(head * HD, (head + 1) * HD), slice(head * slots, (head + 1) * slots)
        q_ref, g_ref, own = parts(head)
        for chunk in range(tokens // CHUNK):
            part = slice(chunk * CHUNK, (chunk + 1) * CHUNK)
            scores = nt(key_ref[:, at], q_ref[part, own]) + bias
            grad_scores = nt(value_ref[:, at], g_ref[part, own])
            top = jnp.max(scores, axis=0, keepdims=True)
            exponent = jnp.exp2((scores - top) * (SCALE * LOG2E))
            attention = exponent * (real[:, part] / jnp.sum(exponent, axis=0, keepdims=True))
            delta = jnp.sum(attention * grad_scores, axis=0, keepdims=True)
            sg_ref[here, part] = (attention * (grad_scores - delta)).astype(jnp.bfloat16)
            att_ref[head % 4, :, part] = attention.astype(jnp.bfloat16)

    def product(head):
        at, here = slice(head * HD, (head + 1) * HD), slice(head * slots, (head + 1) * slots)
        q_ref, g_ref, own = parts(head)
        kg_ref[:, at] = (nn(sg_ref[here, :], q_ref[:, own]) * SCALE).astype(jnp.bfloat16)
        vg_ref[:, at] = nn(att_ref[head % 4], g_ref[:, own]).astype(jnp.bfloat16)

    project(0)
    for head in range(heads):
        if head % 2 == 0 and head + 2 < heads:
            project(head // 2 + 1)
        softmax(head)
        if head > 0:
            product(head - 1)
    product(heads - 1)
    key_weight = jnp.concatenate([block[0][...] for block in blocks], axis=1)
    value_weight = jnp.concatenate([block[1][...] for block in blocks], axis=1)
    partial = nt(kg_ref[...], key_weight) + nt(vg_ref[...], value_weight)
    keep_ref[...] = partial[:half]
    send_ref[...] = partial[half:].astype(jnp.bfloat16)


def attention_call(near, far, gain, bias, real, loaded):
    half, width = near.shape
    slots = 2 * half
    tokens = loaded[2].shape[0]
    columns = sum(x.shape[1] for x in loaded[::4])
    heads = columns // HD
    scratch = lambda *shape: pltpu.VMEM(shape, jnp.bfloat16)
    operands = [near, far, gain, bias, real, *loaded]
    return pl.pallas_call(
        functools.partial(attention_kernel, len(loaded) // 4),
        in_specs=[IN_VMEM] * len(operands),
        out_specs=[IN_VMEM] * 4,
        out_shape=[
            pltpu.VMEM((half, width), jnp.bfloat16),
            pltpu.VMEM((half, width), jnp.float32),
            pltpu.VMEM((heads * slots, tokens), jnp.bfloat16),
            pltpu.VMEM((slots, columns), jnp.bfloat16),
        ],
        scratch_shapes=[
            scratch(slots, columns),
            scratch(4, slots, tokens),
            scratch(slots, columns),
            scratch(slots, columns),
        ],
        compiler_params=small_vmem(8 + 2 * slots * columns * 10 // 2**20),
        name="attention_backward",
    )(*[to_vmem(x) for x in operands])


def query_kernel(first, heads, sg_ref, key_ref, *refs):
    out_ref, block_ref, sems = refs[-3:]
    slots = key_ref.shape[0]
    copies = []
    for index in range(heads):
        head = first + index
        at, here = slice(head * HD, (head + 1) * HD), slice(head * slots, (head + 1) * slots)
        block_ref[index] = (tn(sg_ref[here, :], key_ref[:, at]) * SCALE).astype(jnp.bfloat16)
        copies.append(pltpu.make_async_copy(block_ref.at[index], out_ref.at[:, at], sems.at[index]))
        copies[-1].start()
    for copy in copies:
        copy.wait()


def query_call(first, heads, score_grad, keys, so_far):
    columns = keys.shape[1]
    tokens = score_grad.shape[1]
    before = [] if so_far is None else [so_far]
    return pl.pallas_call(
        functools.partial(query_kernel, first, heads),
        in_specs=[IN_VMEM] * 2 + [pl.BlockSpec(memory_space=pl.ANY)] * len(before),
        out_specs=pl.BlockSpec(memory_space=pl.ANY),
        out_shape=jax.ShapeDtypeStruct((tokens, columns), jnp.bfloat16),
        scratch_shapes=[
            pltpu.VMEM((heads, tokens, HD), jnp.bfloat16),
            pltpu.SemaphoreType.DMA((heads,)),
        ],
        input_output_aliases={2: 0} if before else {},
        compiler_params=small_vmem(8),
        name="query_grad",
    )(to_vmem(score_grad), to_vmem(keys), *before)


def norm_kernel(own_ref, other_ref, hid_ref, gain_ref, out_ref):
    norm_grad = own_ref[...] + other_ref[...].astype(jnp.float32)
    normed, inverse_rms = hid_ref[0], hid_ref[1]
    scaled = norm_grad * gain_ref[...]
    inner_mean = jnp.mean(scaled * normed, axis=-1, keepdims=True)
    out_ref[...] = (inverse_rms * (scaled - normed * inner_mean)).astype(jnp.bfloat16)


def shards(size, queries, out_grad, query_mask, enc_hidden, norm_gain, key_weight, value_weight, mem_len):
    rows, width = enc_hidden.shape
    bits = size.bit_length() - 1
    heads = queries.shape[1] // HD
    arrays = (key_weight, value_weight, queries, out_grad)
    small = (mem_len, query_mask.reshape(1, -1), norm_gain, enc_hidden)
    early = [
        functools.partial(setup_call, rows, bits, size * rows, 0, WIDE, *small),
        functools.partial(load_call, 1 * WIDE, 3 * WIDE),
        functools.partial(load_call, 4 * WIDE, queries.shape[1] - 4 * WIDE),
    ]
    ready = []
    near = enc_hidden
    for step in range(bits - 1):
        last = step == bits - 2
        far = exchange(near, distances(size)[step], size)
        others = [exchange(near, d ^ distances(size)[bits - 1], size) for d in (0, distances(size)[step])] if last else []
        if step < len(early):
            given = lax.optimization_barrier((near, arrays))[1] if step else arrays
            far, others, made = lax.optimization_barrier((far, others, early[step](*given)))
            ready += made
        near = lax.optimization_barrier(jnp.concatenate([near, far], axis=0))
    far = lax.optimization_barrier(jnp.concatenate(others, axis=0))
    bias, real, gain, hidden, *loaded = ready
    send, keep, score_grad, keys = attention_call(near, far, gain, bias, real, loaded)
    query_grad = None
    shares = [(1, 0, 6), (2, 6, 5), (3, 11, 5)]
    for bit in range(bits):
        received = exchange(send, distances(size)[bits - 1 - bit], size)
        for at, first, count in shares:
            if at == bit:
                score_grad, send = lax.optimization_barrier((score_grad, send))
                query_grad = query_call(first, count, score_grad, keys, query_grad)
                received, query_grad = lax.optimization_barrier((received, query_grad))
        if bit < bits - 1:
            half = keep.shape[0] // 2
            total = keep + received.astype(jnp.float32)
            keep, send = total[:half], total[half:].astype(jnp.bfloat16)
    operands = [keep, received, hidden, gain]
    hidden_grad = pl.pallas_call(
        norm_kernel,
        in_specs=[IN_VMEM] * 4,
        out_specs=IN_VMEM,
        out_shape=jax.ShapeDtypeStruct((rows, width), jnp.bfloat16),
        compiler_params=small_vmem(2),
        name="norm_backward",
    )(*[to_vmem(x) for x in operands])
    return (query_grad, hidden_grad)


def solution(mesh):
    in_specs = (
        P(("parts", "seq"), None),
        P(("parts", "seq"), None),
        P(("parts", "seq")),
        P(("parts", "seq"), None),
        P(),
        P(),
        P(),
        P("parts"),
    )
    out_specs = (P(("parts", "seq"), None), P(("parts", "seq"), None))
    body = functools.partial(shards, mesh.shape["seq"])
    return jax.shard_map(body, mesh=mesh, in_specs=in_specs, out_specs=out_specs, check_vma=False)
```
